32 devices in a mesh: date: 8 (over z, x), az: 4 (over y, core).
Axes of the slice: x: 2, y: 2, z: 4, core: 2. Of those that a mesh axis runs over, the one named last changes fastest.
Arguments:
- slc: float32 [48, 2, 32, 1024], P('date', None, 'az'), may hold values from -12 to 12
- pairs: int32 [2, 512, 2], replicated, may hold values from 0 to 47, as said below
Outputs:
- interferogram: float32 [2, 512, 2, 8, 64], P(None, 'date', None, 'az')
- coherence: float32 [2, 512, 8, 64], P(None, 'date', 'az')
The draws below stay inside these ranges and needn't reach their ends.
Inputs may be any that keep to these rules, and one draw needn't show every extreme that they name: In each round the two dates of a pair differ; the pairs in the block of 64 rows of one device name exactly 8 distinct dates, and at most 2 distinct dates out of any one block of 6 dates, exactly 2 out of some block.
All inputs are finite; a program needn't handle non-finite values.
Results may differ from the reference program's by a relative error of at most 0.0014.
Values may be sent and summed in bfloat16 or wider, within the bound.
A program may use at most 64 MiB of HBM per device.

```python
import math
import jax
import jax.numpy as jnp
from jax import lax

RANGE = 1024
DATE_DEV = 6
PAIR_DEV = 64
CAP = 2
ROUNDS = 2
DATES = 48
PAIRS = 512
AZ = 32


def draw_slc(key, part):
    keys = jax.random.split(key, 9)
    scene_re = jax.random.truncated_normal(keys[0], -4.0, 4.0, (AZ, RANGE), jnp.float32)
    scene_im = jax.random.truncated_normal(keys[1], -4.0, 4.0, (AZ, RANGE), jnp.float32)
    amplitude = jnp.exp(jax.random.uniform(keys[2], (AZ, RANGE), jnp.float32, -0.7, 0.7))
    noise = jax.random.truncated_normal(keys[3], -4.0, 4.0, (DATES, 2, AZ, RANGE), jnp.float32)
    sigma = jnp.exp(jax.random.uniform(keys[5], (DATES, 1, 1), jnp.float32, math.log(0.3), math.log(3.0)))
    offset = jax.random.uniform(keys[6], (DATES, 1, 1), jnp.float32, -math.pi, math.pi)
    ramp_range = jax.random.uniform(keys[7], (DATES, 1, 1), jnp.float32, -0.03, 0.03)
    ramp_az = jax.random.uniform(keys[8], (DATES, 1, 1), jnp.float32, -0.1, 0.1)
    cols = jnp.arange(RANGE, dtype=jnp.float32)[None, None, :]
    lines = jnp.arange(AZ, dtype=jnp.float32)[None, :, None]
    phase = offset + ramp_range * cols + ramp_az * lines
    norm_factor = 1.0 / jnp.sqrt(1.0 + sigma * sigma)
    base_re = (scene_re[None] * amplitude[None] + sigma * noise[:, 0]) * norm_factor
    base_im = (scene_im[None] * amplitude[None] + sigma * noise[:, 1]) * norm_factor
    cosine = jnp.cos(phase)
    sine = jnp.sin(phase)
    out_re = jnp.clip(cosine * base_re - sine * base_im, -12.0, 12.0)
    out_im = jnp.clip(sine * base_re + cosine * base_im, -12.0, 12.0)
    return jnp.stack([out_re, out_im], axis=1).astype(jnp.float32)


def pair_block(block_key):
    device_count = PAIRS // PAIR_DEV
    slot_count = device_count * CAP
    used_count = slot_count // 2
    keys = jax.random.split(block_key, 6)
    favoured = jax.random.randint(keys[0], (), 0, device_count)
    shuffled = jax.random.permutation(keys[1], slot_count).astype(jnp.int32)
    slot_index = jnp.arange(slot_count, dtype=jnp.int32)
    slot_source = slot_index // CAP
    scores = jnp.where(slot_source == favoured, slot_index - slot_count, shuffled)
    chosen = jnp.argsort(scores, stable=True)[:used_count]
    source_keys = jax.random.split(keys[2], device_count)
    local_order = jax.vmap(lambda each_key: jax.random.permutation(each_key, DATE_DEV))(source_keys).astype(jnp.int32)
    slot_local = local_order[slot_source, slot_index % CAP]
    slot_date = slot_source * DATE_DEV + slot_local
    dates = slot_date[chosen]
    pair_index = jnp.arange(PAIR_DEV, dtype=jnp.int32)
    covering = pair_index < used_count // 2
    first = jnp.where(covering, 2 * pair_index, jax.random.randint(keys[3], (PAIR_DEV,), 0, used_count))
    stride = jax.random.randint(keys[4], (PAIR_DEV,), 1, used_count)
    second = jnp.where(covering, 2 * pair_index + 1, (first + stride) % used_count)
    order = jax.random.permutation(keys[5], PAIR_DEV)
    listed = jnp.stack([dates[first], dates[second]], axis=-1)
    return listed[order].astype(jnp.int32)


def draw_pairs(key, part):
    device_count = PAIRS // PAIR_DEV
    block_keys = jax.vmap(lambda index: jax.random.fold_in(key, index))(jnp.arange(ROUNDS * device_count))
    blocks = jax.vmap(pair_block)(block_keys)
    return blocks.reshape(ROUNDS, PAIRS, 2).astype(jnp.int32)


def setup_inputs(seed: int = 0) -> dict:
    key_of = jax.random.split(jax.random.key(seed), 3)
    slc = draw_slc(jax.random.fold_in(key_of[2], 71), 0)
    pairs = draw_pairs(jax.random.fold_in(key_of[2], 71), 0)
    return dict(slc=slc, pairs=pairs)


def multilook(field):
    shape = field.shape
    blocks = field.reshape(shape[:-2] + (shape[-2] // 4, 4, shape[-1] // 16, 16))
    return blocks.mean(axis=(-3, -1))

def pair_looks(first, second):
    first_re, first_im = (first[0], first[1])
    second_re, second_im = (second[0], second[1])
    prod_re = first_re * second_re + first_im * second_im
    prod_im = first_im * second_re - first_re * second_im
    power_a = first_re * first_re + first_im * first_im
    power_b = second_re * second_re + second_im * second_im
    return jnp.stack([multilook(prod_re), multilook(prod_im), multilook(power_a), multilook(power_b)], axis=0)

def coherence_from(padded):
    lines = padded.shape[-2] - 4
    columns = padded.shape[-1]
    az_sum = padded[..., 0:lines, :]
    for offset in range(1, 5):
        az_sum = az_sum + padded[..., offset:offset + lines, :]
    widths = [(0, 0)] * (az_sum.ndim - 1) + [(2, 2)]
    wide = jnp.pad(az_sum, widths)
    boxed = wide[..., 0:columns]
    for offset in range(1, 5):
        boxed = boxed + wide[..., offset:offset + columns]
    numer = jnp.sqrt(boxed[..., 0, :, :] ** 2 + boxed[..., 1, :, :] ** 2)
    return numer / jnp.sqrt(boxed[..., 2, :, :] * boxed[..., 3, :, :])

def reference(slc, pairs):
    quantized = lax.optimization_barrier(slc.astype(jnp.bfloat16))
    flat_pairs = pairs.reshape(-1, 2)

    def one_pair(pair_row):
        first = lax.dynamic_index_in_dim(quantized, pair_row[0], 0, keepdims=False).astype(jnp.float32)
        second = lax.dynamic_index_in_dim(quantized, pair_row[1], 0, keepdims=False).astype(jnp.float32)
        looks = pair_looks(first, second)
        padded = jnp.pad(looks, ((0, 0), (2, 2), (0, 0)))
        return (looks[0:2], coherence_from(padded))
    ifg_all, coh_all = lax.map(one_pair, flat_pairs)
    ifg_all = ifg_all.reshape((ROUNDS, PAIRS) + ifg_all.shape[1:])
    coh_all = coh_all.reshape((ROUNDS, PAIRS) + coh_all.shape[1:])
    return (ifg_all, coh_all)
```

```python
import jax
import jax.numpy as jnp
from jax import lax
from jax.experimental import pallas as pl
from jax.experimental.pallas import tpu as pltpu
from jax.sharding import PartitionSpec as P

CAP = 2


def with_halo(shard, sides, width):
    for axis, dim in sides:
        peers, length = (lax.axis_size(axis), shard.shape[dim])
        up = [(i, (i + 1) % peers) for i in range(peers - 1)]
        down = [(j, i) for i, j in up]
        last = lax.slice_in_dim(shard, length - width, length, axis=dim)
        first = lax.slice_in_dim(shard, 0, width, axis=dim)
        before = lax.ppermute(last, axis, up)
        after = lax.ppermute(first, axis, down)
        shard = jnp.concatenate([before, shard, after], axis=dim)
    return shard


def multilook(field):
    shape = field.shape
    blocks = field.reshape(shape[:-2] + (shape[-2] // 4, 4, shape[-1] // 16, 16))
    return blocks.mean(axis=(-3, -1))


def pair_looks(tiles):
    first = tiles[:, 0].astype(jnp.float32)
    second = tiles[:, 1].astype(jnp.float32)
    first_re, first_im = (first[:, 0], first[:, 1])
    second_re, second_im = (second[:, 0], second[:, 1])
    prod_re = first_re * second_re + first_im * second_im
    prod_im = first_im * second_re - first_re * second_im
    power_a = first_re * first_re + first_im * first_im
    power_b = second_re * second_re + second_im * second_im
    return jnp.stack(
        [multilook(prod_re), multilook(prod_im), multilook(power_a), multilook(power_b)], axis=1
    )


def coherence_from(padded):
    lines = padded.shape[-2] - 4
    columns = padded.shape[-1]
    az_sum = padded[..., 0:lines, :]
    for offset in range(1, 5):
        az_sum = az_sum + padded[..., offset : offset + lines, :]
    widths = [(0, 0)] * (az_sum.ndim - 1) + [(2, 2)]
    wide = jnp.pad(az_sum, widths)
    boxed = wide[..., 0:columns]
    for offset in range(1, 5):
        boxed = boxed + wide[..., offset : offset + columns]
    numer = jnp.sqrt(boxed[..., 0, :, :] ** 2 + boxed[..., 1, :, :] ** 2)
    return numer / jnp.sqrt(boxed[..., 2, :, :] * boxed[..., 3, :, :])


def per_device_general(slc, pairs):
    date_count = lax.axis_size("date")
    own_index = lax.axis_index("date")
    date_dev = slc.shape[0]
    pair_dev = pairs.shape[1] // date_count
    tile_shape = slc.shape[1:]
    quantized = lax.optimization_barrier(slc.astype(jnp.bfloat16))
    all_ids = jnp.arange(date_count * date_dev, dtype=jnp.int32)
    local_ids = own_index * date_dev + jnp.arange(date_dev, dtype=jnp.int32)
    local_pos = jnp.arange(date_dev, dtype=jnp.int32)
    slot_ids = jnp.arange(CAP, dtype=jnp.int32)
    looks_list = []
    for round_index in range(pairs.shape[0]):
        block = pairs[round_index]
        own_pairs = lax.dynamic_slice_in_dim(block, own_index * pair_dev, pair_dev, 0)
        entries = own_pairs.reshape(-1)
        wanted = block.reshape(date_count, 2 * pair_dev)
        needed = jnp.any(wanted[:, :, None] == local_ids[None, None, :], axis=1).astype(jnp.int32)
        ranks = jnp.cumsum(needed, axis=1) - needed
        picked = needed[:, None, :] * (ranks[:, None, :] == slot_ids[None, :, None]).astype(
            jnp.int32
        )
        source_local = jnp.sum(picked * local_pos[None, None, :], axis=2)
        present = jnp.sum(picked, axis=2) > 0
        outgoing = jnp.take(quantized, source_local.reshape(-1), axis=0).reshape(
            (date_count, CAP) + tile_shape
        )
        outgoing = jnp.where(present[:, :, None, None, None], outgoing, jnp.zeros((), jnp.bfloat16))
        incoming = lax.all_to_all(outgoing, "date", split_axis=0, concat_axis=0, tiled=True)
        matches = entries[:, None] == all_ids[None, :]
        my_need = jnp.any(matches, axis=0).astype(jnp.int32).reshape(date_count, date_dev)
        my_rank = (jnp.cumsum(my_need, axis=1) - my_need).reshape(-1)
        entry_slot = jnp.sum(jnp.where(matches, my_rank[None, :], 0), axis=1)
        position = entries // date_dev * CAP + entry_slot
        fetched = jnp.take(incoming.reshape((date_count * CAP,) + tile_shape), position, axis=0)
        looks = pair_looks(fetched.reshape((pair_dev, 2) + tile_shape))
        looks_list.append(looks)
    stacked = jnp.stack(looks_list, axis=0)
    padded = with_halo(stacked, (("az", 3),), 2)
    coherence = coherence_from(padded)
    interferogram = stacked[:, :, 0:2]
    return (interferogram, coherence)


LINES, SAMPLES = 4, 16
STEPS = ((0, 2), (0, 1), (1, 8), (1, 4), (1, 2), (1, 1))


def iota(shape, dim):
    return lax.broadcasted_iota(jnp.int32, shape, dim)


def place_of(leaf):
    bit = [(leaf >> n) & 1 for n in range(6)]
    return 32 * bit[3] + 16 * bit[4] + 8 * bit[5] + 4 * bit[2] + 2 * bit[0] + bit[1]


def rolled(x, shift, dim):
    return pltpu.roll(x, shift % x.shape[dim], dim)


def join(one, two, dim, dist):
    low = (iota(one.shape, dim) & dist) == 0
    kept = jnp.where(low, one, two)
    other = jnp.where(low, two, one)
    return kept + jnp.where(low, rolled(other, -dist, dim), rolled(other, dist, dim))


def cell_sums(real, imag):
    count = len(real)
    couples = [(i, j) for i in range(count) for j in range(i + 1, count)]

    def quantity(place):
        if place < len(couples):
            i, j = couples[place]
            return real[i] * real[j] + imag[i] * imag[j]
        place -= len(couples)
        if place < len(couples):
            i, j = couples[place]
            return imag[i] * real[j] - real[i] * imag[j]
        i = place - len(couples)
        return real[i] * real[i] + imag[i] * imag[i]

    def build(level, base):
        if level == 0:
            return quantity(place_of(base))
        one = build(level - 1, base)
        two = build(level - 1, base + (1 << (level - 1)))
        return join(one, two, *STEPS[level - 1])

    return build(len(STEPS), 0)


def exact_dot(a, b):
    return lax.dot_general(
        a,
        b,
        (((1,), (0,)), ((), ())),
        precision=lax.Precision.HIGHEST,
        preferred_element_type=jnp.float32,
    )


def cells_last(x):
    shape = (128, 128)
    src, dst = iota(shape, 0), iota(shape, 1)
    hit = dst == (src % SAMPLES) * (128 // SAMPLES) + src // SAMPLES
    return exact_dot(x, jnp.where(hit, 1.0 / (LINES * SAMPLES), 0.0).astype(jnp.float32))


def table_of(tiles):
    lane, sub = iota((8, 128), 1), iota((8, 128), 0)
    tiles = list(tiles)
    for b in range(3):
        dist = 8 << b
        low = (lane & dist) == 0
        for j in range(8):
            if not j >> b & 1:
                one, two = tiles[j], tiles[j | 1 << b]
                tiles[j] = jnp.where(low, one, rolled(two, dist, 1))
                tiles[j | 1 << b] = jnp.where(low, rolled(one, -dist, 1), two)
    same = (sub < 4) == (lane < 64)
    return [jnp.where(same, t, rolled(rolled(t, 4, 0), 64, 1)) for t in tiles]


def box_of(own, before, after):
    lane = iota(own.shape, 1)
    first = lane < 64
    both = own + rolled(own, 64, 1)
    both = both + jnp.where(first, before + rolled(before, 64, 1), before)
    both = both + jnp.where(first, after, after + rolled(after, 64, 1))
    cell = lane & 63
    out = both
    for o in (-2, -1, 1, 2):
        valid = (cell + o >= 0) & (cell + o < 64)
        out = out + jnp.where(valid, rolled(both, -o, 1), 0.0)
    return out


def expand(looks, boxed, rank_a, rank_b, count):
    rows = rank_a.shape[0]
    total = looks.shape[0]
    q = iota((rows, total), 1)
    low, high = jnp.minimum(rank_a, rank_b), jnp.maximum(rank_a, rank_b)
    place = ((low * (2 * count - 1 - low)) >> 1) + high - low - 1
    couples = count * (count - 1) // 2
    sel_re = jnp.where(q == place, 1.0, 0.0)
    sel_im = jnp.where(q == place + couples, jnp.where(rank_a < rank_b, 1.0, -1.0), 0.0)
    sel_a = jnp.where(q == rank_a + 2 * couples, 1.0, 0.0)
    sel_b = jnp.where(q == rank_b + 2 * couples, 1.0, 0.0)
    means = exact_dot(jnp.concatenate([sel_re, sel_im], 0), looks)
    sums = exact_dot(jnp.concatenate([sel_re, sel_im, sel_a, sel_b], 0), boxed)
    box_re, box_im, box_a, box_b = (sums[n * rows : (n + 1) * rows] for n in range(4))
    coherence = jnp.sqrt(box_re * box_re + box_im * box_im) / jnp.sqrt(box_a * box_b)
    return means[:rows], means[rows:], coherence


def sums_kernel(ids_ref, all_ref, out_ref, packed):
    groups, dates = ids_ref.shape

    def step(group, carry):
        real, imag = [], []
        for k in range(dates):
            date = ids_ref[group, k]
            real.append(all_ref[date, 0].astype(jnp.float32))
            imag.append(all_ref[date, 1].astype(jnp.float32))
        packed[pl.ds(pl.multiple_of(group * 8, 8), 8), :] = cell_sums(real, imag)
        return carry

    lax.fori_loop(0, groups, step, 0)
    out_ref[...] = cells_last(packed[...])


def table_kernel(in_ref, out_ref):
    for r in range(in_ref.shape[1]):
        for k, tile in enumerate(table_of([in_ref[j, r] for j in range(8)])):
            out_ref[r, 8 * k : 8 * k + 8, :] = tile


def final_kernel(own_ref, before_ref, after_ref, ranks_ref, ifg_ref, coh_ref):
    for r in range(own_ref.shape[0]):
        looks = own_ref[r]
        boxed = box_of(looks, before_ref[r], after_ref[r])
        ranks = ranks_ref[r]
        mean_re, mean_im, coherence = expand(looks, boxed, ranks[:, 0:1], ranks[:, 1:2], 8)
        ifg_ref[r, :, 0, :] = mean_re
        ifg_ref[r, :, 1, :] = mean_im
        coh_ref[r] = coherence


def plan(pairs, own_index, peers, dates):
    rounds = pairs.shape[0]
    pair_dev = pairs.shape[1] // peers
    all_ids = jnp.arange(dates, dtype=jnp.int32)
    wanted = pairs.reshape(rounds, peers, 2 * pair_dev)
    needed = jnp.any(wanted[:, :, :, None] == all_ids, axis=2)
    before = (all_ids[:, None] < all_ids[None, :])
    rank = jnp.sum((needed[:, :, :, None] & before).astype(jnp.int32), axis=2)
    slots = jnp.arange(peers, dtype=jnp.int32)
    hit = needed[:, :, None, :] & (rank[:, :, None, :] == slots[None, None, :, None])
    ids = jnp.sum(jnp.where(hit, all_ids, 0), axis=3)
    own = lax.dynamic_slice_in_dim(pairs, own_index * pair_dev, pair_dev, 1)
    own_needed = jnp.any((own[:, :, :, None] == all_ids).reshape(rounds, -1, dates), axis=1)
    smaller = own_needed[:, None, None, :] & (all_ids < own[..., None])
    ranks = jnp.sum(smaller.astype(jnp.int32), axis=3)
    return ids.transpose(1, 0, 2).reshape(peers * rounds, peers), ranks


def per_device_few(slc, pairs):
    peers = lax.axis_size("date")
    rounds = pairs.shape[0]
    pair_dev = pairs.shape[1] // peers
    date_dev, _, lines, columns = slc.shape
    ids, ranks = plan(pairs, lax.axis_index("date"), peers, date_dev * peers)
    sent = slc.astype(jnp.bfloat16).reshape(date_dev, 2, lines, peers, columns // peers)
    sent = sent.transpose(3, 0, 1, 2, 4)
    held = lax.all_to_all(sent, "date", split_axis=0, concat_axis=0, tiled=True)
    held = held.reshape(peers * date_dev, 2, lines, columns // peers)
    vmem = pl.BlockSpec(memory_space=pltpu.VMEM)
    sums = pl.pallas_call(
        sums_kernel,
        out_shape=jax.ShapeDtypeStruct((peers * rounds * 8, 128), jnp.float32),
        in_specs=[pl.BlockSpec(memory_space=pltpu.SMEM), vmem],
        out_specs=vmem,
        scratch_shapes=[pltpu.VMEM((peers * rounds * 8, 128), jnp.float32)],
    )(ids, held)
    sums = sums.reshape(peers, rounds, 8, 128)
    tiles = lax.all_to_all(sums, "date", split_axis=0, concat_axis=0, tiled=True)
    table = pl.pallas_call(
        table_kernel,
        out_shape=jax.ShapeDtypeStruct((rounds, 64, 128), jnp.float32),
        in_specs=[vmem],
        out_specs=vmem,
    )(tiles)
    az = lax.axis_size("az")
    up = [(i, i + 1) for i in range(az - 1)]
    before = lax.ppermute(table, "az", up)
    after = lax.ppermute(table, "az", [(j, i) for i, j in up])
    ifg, coh = pl.pallas_call(
        final_kernel,
        out_shape=(
            jax.ShapeDtypeStruct((rounds, pair_dev, 2, 128), jnp.float32),
            jax.ShapeDtypeStruct((rounds, pair_dev, 128), jnp.float32),
        ),
        in_specs=[vmem] * 4,
        out_specs=(vmem, vmem),
    )(table, before, after, ranks)
    cells = columns // SAMPLES
    return (
        ifg.reshape(rounds, pair_dev, 2, lines // LINES, cells),
        coh.reshape(rounds, pair_dev, lines // LINES, cells),
    )


def per_device(slc, pairs):
    peers = lax.axis_size("date")
    lines, columns = slc.shape[2:]
    few = peers == 8 and (lines, columns) == (2 * LINES, 64 * SAMPLES)
    return per_device_few(slc, pairs) if few else per_device_general(slc, pairs)


def solution(mesh):
    return jax.shard_map(
        per_device,
        mesh=mesh,
        in_specs=(P("date", None, "az", None), P()),
        out_specs=(P(None, "date", None, "az", None), P(None, "date", "az", None)),
        check_vma=False,
    )
```

```python
import jax
import jax.numpy as jnp
from jax import lax
from jax.experimental import pallas as pl
from jax.experimental.pallas import tpu as pltpu
from jax.sharding import PartitionSpec as P

CAP = 2


def with_halo(shard, sides, width):
    for axis, dim in sides:
        peers, length = (lax.axis_size(axis), shard.shape[dim])
        up = [(i, (i + 1) % peers) for i in range(peers - 1)]
        down = [(j, i) for i, j in up]
        last = lax.slice_in_dim(shard, length - width, length, axis=dim)
        first = lax.slice_in_dim(shard, 0, width, axis=dim)
        before = lax.ppermute(last, axis, up)
        after = lax.ppermute(first, axis, down)
        shard = jnp.concatenate([before, shard, after], axis=dim)
    return shard


def multilook(field):
    shape = field.shape
    blocks = field.reshape(shape[:-2] + (shape[-2] // 4, 4, shape[-1] // 16, 16))
    return blocks.mean(axis=(-3, -1))


def pair_looks(tiles):
    first = tiles[:, 0].astype(jnp.float32)
    second = tiles[:, 1].astype(jnp.float32)
    first_re, first_im = (first[:, 0], first[:, 1])
    second_re, second_im = (second[:, 0], second[:, 1])
    prod_re = first_re * second_re + first_im * second_im
    prod_im = first_im * second_re - first_re * second_im
    power_a = first_re * first_re + first_im * first_im
    power_b = second_re * second_re + second_im * second_im
    return jnp.stack(
        [multilook(prod_re), multilook(prod_im), multilook(power_a), multilook(power_b)], axis=1
    )


def coherence_from(padded):
    lines = padded.shape[-2] - 4
    columns = padded.shape[-1]
    az_sum = padded[..., 0:lines, :]
    for offset in range(1, 5):
        az_sum = az_sum + padded[..., offset : offset + lines, :]
    widths = [(0, 0)] * (az_sum.ndim - 1) + [(2, 2)]
    wide = jnp.pad(az_sum, widths)
    boxed = wide[..., 0:columns]
    for offset in range(1, 5):
        boxed = boxed + wide[..., offset : offset + columns]
    numer = jnp.sqrt(boxed[..., 0, :, :] ** 2 + boxed[..., 1, :, :] ** 2)
    return numer / jnp.sqrt(boxed[..., 2, :, :] * boxed[..., 3, :, :])


def per_device_general(slc, pairs):
    date_count = lax.axis_size("date")
    own_index = lax.axis_index("date")
    date_dev = slc.shape[0]
    pair_dev = pairs.shape[1] // date_count
    tile_shape = slc.shape[1:]
    quantized = lax.optimization_barrier(slc.astype(jnp.bfloat16))
    all_ids = jnp.arange(date_count * date_dev, dtype=jnp.int32)
    local_ids = own_index * date_dev + jnp.arange(date_dev, dtype=jnp.int32)
    local_pos = jnp.arange(date_dev, dtype=jnp.int32)
    slot_ids = jnp.arange(CAP, dtype=jnp.int32)
    looks_list = []
    for round_index in range(pairs.shape[0]):
        block = pairs[round_index]
        own_pairs = lax.dynamic_slice_in_dim(block, own_index * pair_dev, pair_dev, 0)
        entries = own_pairs.reshape(-1)
        wanted = block.reshape(date_count, 2 * pair_dev)
        needed = jnp.any(wanted[:, :, None] == local_ids[None, None, :], axis=1).astype(jnp.int32)
        ranks = jnp.cumsum(needed, axis=1) - needed
        picked = needed[:, None, :] * (ranks[:, None, :] == slot_ids[None, :, None]).astype(
            jnp.int32
        )
        source_local = jnp.sum(picked * local_pos[None, None, :], axis=2)
        present = jnp.sum(picked, axis=2) > 0
        outgoing = jnp.take(quantized, source_local.reshape(-1), axis=0).reshape(
            (date_count, CAP) + tile_shape
        )
        outgoing = jnp.where(present[:, :, None, None, None], outgoing, jnp.zeros((), jnp.bfloat16))
        incoming = lax.all_to_all(outgoing, "date", split_axis=0, concat_axis=0, tiled=True)
        matches = entries[:, None] == all_ids[None, :]
        my_need = jnp.any(matches, axis=0).astype(jnp.int32).reshape(date_count, date_dev)
        my_rank = (jnp.cumsum(my_need, axis=1) - my_need).reshape(-1)
        entry_slot = jnp.sum(jnp.where(matches, my_rank[None, :], 0), axis=1)
        position = entries // date_dev * CAP + entry_slot
        fetched = jnp.take(incoming.reshape((date_count * CAP,) + tile_shape), position, axis=0)
        looks = pair_looks(fetched.reshape((pair_dev, 2) + tile_shape))
        looks_list.append(looks)
    stacked = jnp.stack(looks_list, axis=0)
    padded = with_halo(stacked, (("az", 3),), 2)
    coherence = coherence_from(padded)
    interferogram = stacked[:, :, 0:2]
    return (interferogram, coherence)


LINES, SAMPLES = 4, 16
STEPS = ((0, 2), (0, 1), (1, 8), (1, 4), (1, 2), (1, 1))


def iota(shape, dim):
    return lax.broadcasted_iota(jnp.int32, shape, dim)


def place_of(leaf):
    bit = [(leaf >> n) & 1 for n in range(6)]
    return 32 * bit[3] + 16 * bit[4] + 8 * bit[5] + 4 * bit[2] + 2 * bit[0] + bit[1]


def rolled(x, shift, dim):
    return pltpu.roll(x, shift % x.shape[dim], dim)


def join(one, two, dim, dist):
    low = (iota(one.shape, dim) & dist) == 0
    kept = jnp.where(low, one, two)
    other = jnp.where(low, two, one)
    return kept + jnp.where(low, rolled(other, -dist, dim), rolled(other, dist, dim))


def cell_sums(real, imag):
    count = len(real)
    couples = [(i, j) for i in range(count) for j in range(i + 1, count)]

    def quantity(place):
        if place < len(couples):
            i, j = couples[place]
            return real[i] * real[j] + imag[i] * imag[j]
        place -= len(couples)
        if place < len(couples):
            i, j = couples[place]
            return imag[i] * real[j] - real[i] * imag[j]
        i = place - len(couples)
        return real[i] * real[i] + imag[i] * imag[i]

    def build(level, base):
        if level == 0:
            return quantity(place_of(base))
        one = build(level - 1, base)
        two = build(level - 1, base + (1 << (level - 1)))
        return join(one, two, *STEPS[level - 1])

    return build(len(STEPS), 0)


def exact_dot(a, b):
    return lax.dot_general(
        a,
        b,
        (((1,), (0,)), ((), ())),
        precision=lax.Precision.HIGHEST,
        preferred_element_type=jnp.float32,
    )


def cells_last(x):
    shape = (128, 128)
    src, dst = iota(shape, 0), iota(shape, 1)
    hit = dst == (src % SAMPLES) * (128 // SAMPLES) + src // SAMPLES
    return exact_dot(x, jnp.where(hit, 1.0 / (LINES * SAMPLES), 0.0).astype(jnp.float32))


def table_of(tiles):
    lane, sub = iota((8, 128), 1), iota((8, 128), 0)
    tiles = list(tiles)
    for b in range(3):
        dist = 8 << b
        low = (lane & dist) == 0
        for j in range(8):
            if not j >> b & 1:
                one, two = tiles[j], tiles[j | 1 << b]
                tiles[j] = jnp.where(low, one, rolled(two, dist, 1))
                tiles[j | 1 << b] = jnp.where(low, rolled(one, -dist, 1), two)
    same = (sub < 4) == (lane < 64)
    return [jnp.where(same, t, rolled(rolled(t, 4, 0), 64, 1)) for t in tiles]


def box_of(own, before, after):
    lane = iota(own.shape, 1)
    first = lane < 64
    both = own + rolled(own, 64, 1)
    both = both + jnp.where(first, before + rolled(before, 64, 1), before)
    both = both + jnp.where(first, after, after + rolled(after, 64, 1))
    cell = lane & 63
    out = both
    for o in (-2, -1, 1, 2):
        valid = (cell + o >= 0) & (cell + o < 64)
        out = out + jnp.where(valid, rolled(both, -o, 1), 0.0)
    return out


def expand(looks, boxed, rank_a, rank_b, count):
    rows = rank_a.shape[0]
    total = looks.shape[0]
    q = iota((rows, total), 1)
    low, high = jnp.minimum(rank_a, rank_b), jnp.maximum(rank_a, rank_b)
    place = ((low * (2 * count - 1 - low)) >> 1) + high - low - 1
    couples = count * (count - 1) // 2
    sel_re = jnp.where(q == place, 1.0, 0.0)
    sel_im = jnp.where(q == place + couples, jnp.where(rank_a < rank_b, 1.0, -1.0), 0.0)
    sel_a = jnp.where(q == rank_a + 2 * couples, 1.0, 0.0)
    sel_b = jnp.where(q == rank_b + 2 * couples, 1.0, 0.0)
    means = exact_dot(jnp.concatenate([sel_re, sel_im], 0), looks)
    sums = exact_dot(jnp.concatenate([sel_re, sel_im, sel_a, sel_b], 0), boxed)
    box_re, box_im, box_a, box_b = (sums[n * rows : (n + 1) * rows] for n in range(4))
    coherence = jnp.sqrt(box_re * box_re + box_im * box_im) / jnp.sqrt(box_a * box_b)
    return means[:rows], means[rows:], coherence


MESH = pl.DeviceIdType.MESH


def list_dates(entries, dates, count):
    lane = iota(entries.shape, 1)
    seen = jnp.zeros((entries.shape[0], 1), jnp.int32)
    listed = jnp.zeros(entries.shape, jnp.int32)
    for date in range(dates):
        named = jnp.max((entries == date).astype(jnp.int32), axis=1, keepdims=True)
        listed = jnp.where((lane == seen) & (named > 0), date, listed)
        seen = seen + named
    return listed


def stack_kernel(
    slc_ref,
    pairs_ref,
    entries_ref,
    ifg_ref,
    coh_ref,
    sent,
    held,
    sums,
    tiles,
    table,
    halo,
    listed,
    ids,
    send_a,
    recv_a,
    send_b,
    recv_b,
    send_h,
    recv_h,
    list_sem,
):
    peers, az_size = lax.axis_size("date"), lax.axis_size("az")
    me, az = lax.axis_index("date"), lax.axis_index("az")
    date_dev = slc_ref.shape[0]
    rounds = pairs_ref.shape[0]
    pair_dev = pairs_ref.shape[1] // peers
    width = slc_ref.shape[3] // peers
    sides = ((-1, az > 0), (1, az < az_size - 1))

    barrier = pltpu.get_barrier_semaphore()
    for o in range(1, peers):
        pl.semaphore_signal(
            barrier, inc=1, device_id={"date": lax.rem(me + o, peers)}, device_id_type=MESH
        )
    for step, there in sides:

        @pl.when(there)
        def _():
            pl.semaphore_signal(barrier, inc=1, device_id={"az": az + step}, device_id_type=MESH)

    for j in range(peers):
        sent[j] = slc_ref[:, :, :, j * width : (j + 1) * width].astype(jnp.bfloat16)
    greeted = peers - 1 + (az > 0).astype(jnp.int32) + (az < az_size - 1).astype(jnp.int32)
    pl.semaphore_wait(barrier, greeted)

    def images(o):
        peer = lax.rem(me + o, peers)
        return pltpu.make_async_remote_copy(
            src_ref=sent.at[peer],
            dst_ref=held.at[me],
            send_sem=send_a.at[o],
            recv_sem=recv_a.at[o],
            device_id={"date": peer},
            device_id_type=MESH,
        )

    for o in range(1, peers):
        images(o).start()
    held[me] = sent[me]
    listed[...] = list_dates(entries_ref[...], date_dev * peers, peers)
    fetch = pltpu.make_async_copy(listed, ids, list_sem)
    fetch.start()
    fetch.wait()
    for o in range(1, peers):
        images(o).wait_recv()

    def results(o):
        peer = lax.rem(me + o, peers)
        return pltpu.make_async_remote_copy(
            src_ref=sums.at[peer],
            dst_ref=tiles.at[me],
            send_sem=send_b.at[o],
            recv_sem=recv_b.at[o],
            device_id={"date": peer},
            device_id_type=MESH,
        )

    def serve(o, carry):
        peer = lax.rem(me + o, peers)
        packed = []
        for r in range(rounds):
            real, imag = [], []
            for k in range(peers):
                date = ids[r * peers + peer, k]
                owner = date // date_dev
                real.append(held[owner, date - owner * date_dev, 0].astype(jnp.float32))
                imag.append(held[owner, date - owner * date_dev, 1].astype(jnp.float32))
            packed.append(cell_sums(real, imag))
        done = cells_last(jnp.concatenate(packed, 0))
        for r in range(rounds):
            sums[peer, r] = done[8 * r : 8 * r + 8]

        @pl.when(o < peers)
        def _():
            results(o).start()

        return carry

    lax.fori_loop(1, peers + 1, serve, 0)
    tiles[me] = sums[me]
    for o in range(1, peers):
        results(o).wait_recv()
    for r in range(rounds):
        for k, tile in enumerate(table_of([tiles[j, r] for j in range(peers)])):
            table[r, 8 * k : 8 * k + 8, :] = tile

    def edge(n, step):
        return pltpu.make_async_remote_copy(
            src_ref=table,
            dst_ref=halo.at[n],
            send_sem=send_h.at[n],
            recv_sem=recv_h.at[n],
            device_id={"az": az + step},
            device_id_type=MESH,
        )

    for n, (step, there) in enumerate(sides):

        @pl.when(there)
        def _():
            edge(n, step).start()

        @pl.when(jnp.logical_not(there))
        def _():
            halo[1 - n] = jnp.zeros_like(halo[1 - n])

    for n, (step, there) in enumerate(sides):

        @pl.when(there)
        def _():
            edge(1 - n, step).wait_recv()

    for r in range(rounds):
        own = pairs_ref[r, pl.ds(pl.multiple_of(me * pair_dev, 8), pair_dev), :]
        ranks = jnp.zeros_like(own)
        for k in range(peers):
            ranks = ranks + (own > ids[r * peers + me, k]).astype(jnp.int32)
        looks = table[r]
        boxed = box_of(looks, halo[1, r], halo[0, r])
        mean_re, mean_im, coherence = expand(looks, boxed, ranks[:, 0:1], ranks[:, 1:2], peers)
        ifg_ref[r, :, 0, :] = mean_re
        ifg_ref[r, :, 1, :] = mean_im
        coh_ref[r] = coherence

    for o in range(1, peers):
        images(o).wait_send()
        results(o).wait_send()
    for n, (step, there) in enumerate(sides):

        @pl.when(there)
        def _():
            edge(n, step).wait_send()


def per_device_few(slc, pairs):
    peers = lax.axis_size("date")
    rounds = pairs.shape[0]
    pair_dev = pairs.shape[1] // peers
    date_dev, _, lines, columns = slc.shape
    width = columns // peers
    entries = pairs.reshape(rounds * peers, 2 * pair_dev)
    vmem = pl.BlockSpec(memory_space=pltpu.VMEM)
    dma = pltpu.SemaphoreType.DMA
    ifg, coh = pl.pallas_call(
        stack_kernel,
        out_shape=(
            jax.ShapeDtypeStruct((rounds, pair_dev, 2, 128), jnp.float32),
            jax.ShapeDtypeStruct((rounds, pair_dev, 128), jnp.float32),
        ),
        in_specs=[vmem] * 3,
        out_specs=(vmem, vmem),
        scratch_shapes=[
            pltpu.VMEM((peers, date_dev, 2, lines, width), jnp.bfloat16),
            pltpu.VMEM((peers, date_dev, 2, lines, width), jnp.bfloat16),
            pltpu.VMEM((peers, rounds, 8, 128), jnp.float32),
            pltpu.VMEM((peers, rounds, 8, 128), jnp.float32),
            pltpu.VMEM((rounds, 64, 128), jnp.float32),
            pltpu.VMEM((2, rounds, 64, 128), jnp.float32),
            pltpu.VMEM(entries.shape, jnp.int32),
            pltpu.SMEM(entries.shape, jnp.int32),
            dma((peers,)),
            dma((peers,)),
            dma((peers,)),
            dma((peers,)),
            dma((2,)),
            dma((2,)),
            dma,
        ],
        compiler_params=pltpu.CompilerParams(collective_id=0, has_side_effects=True),
    )(slc, pairs, entries)
    cells = columns // SAMPLES
    return (
        ifg.reshape(rounds, pair_dev, 2, lines // LINES, cells),
        coh.reshape(rounds, pair_dev, lines // LINES, cells),
    )


def per_device(slc, pairs):
    peers = lax.axis_size("date")
    lines, columns = slc.shape[2:]
    few = peers == 8 and (lines, columns) == (2 * LINES, 64 * SAMPLES)
    return per_device_few(slc, pairs) if few else per_device_general(slc, pairs)


def solution(mesh):
    return jax.shard_map(
        per_device,
        mesh=mesh,
        in_specs=(P("date", None, "az", None), P()),
        out_specs=(P(None, "date", None, "az", None), P(None, "date", "az", None)),
        check_vma=False,
    )
```

```python
import jax
import jax.numpy as jnp
from jax import lax
from jax.experimental import pallas as pl
from jax.experimental.pallas import tpu as pltpu
from jax.sharding import PartitionSpec as P

CAP = 2


def with_halo(shard, sides, width):
    for axis, dim in sides:
        peers, length = (lax.axis_size(axis), shard.shape[dim])
        up = [(i, (i + 1) % peers) for i in range(peers - 1)]
        down = [(j, i) for i, j in up]
        last = lax.slice_in_dim(shard, length - width, length, axis=dim)
        first = lax.slice_in_dim(shard, 0, width, axis=dim)
        before = lax.ppermute(last, axis, up)
        after = lax.ppermute(first, axis, down)
        shard = jnp.concatenate([before, shard, after], axis=dim)
    return shard


def multilook(field):
    shape = field.shape
    blocks = field.reshape(shape[:-2] + (shape[-2] // 4, 4, shape[-1] // 16, 16))
    return blocks.mean(axis=(-3, -1))


def pair_looks(tiles):
    first = tiles[:, 0].astype(jnp.float32)
    second = tiles[:, 1].astype(jnp.float32)
    first_re, first_im = (first[:, 0], first[:, 1])
    second_re, second_im = (second[:, 0], second[:, 1])
    prod_re = first_re * second_re + first_im * second_im
    prod_im = first_im * second_re - first_re * second_im
    power_a = first_re * first_re + first_im * first_im
    power_b = second_re * second_re + second_im * second_im
    return jnp.stack(
        [multilook(prod_re), multilook(prod_im), multilook(power_a), multilook(power_b)], axis=1
    )


def coherence_from(padded):
    lines = padded.shape[-2] - 4
    columns = padded.shape[-1]
    az_sum = padded[..., 0:lines, :]
    for offset in range(1, 5):
        az_sum = az_sum + padded[..., offset : offset + lines, :]
    widths = [(0, 0)] * (az_sum.ndim - 1) + [(2, 2)]
    wide = jnp.pad(az_sum, widths)
    boxed = wide[..., 0:columns]
    for offset in range(1, 5):
        boxed = boxed + wide[..., offset : offset + columns]
    numer = jnp.sqrt(boxed[..., 0, :, :] ** 2 + boxed[..., 1, :, :] ** 2)
    return numer / jnp.sqrt(boxed[..., 2, :, :] * boxed[..., 3, :, :])


def per_device_general(slc, pairs):
    date_count = lax.axis_size("date")
    own_index = lax.axis_index("date")
    date_dev = slc.shape[0]
    pair_dev = pairs.shape[1] // date_count
    tile_shape = slc.shape[1:]
    quantized = lax.optimization_barrier(slc.astype(jnp.bfloat16))
    all_ids = jnp.arange(date_count * date_dev, dtype=jnp.int32)
    local_ids = own_index * date_dev + jnp.arange(date_dev, dtype=jnp.int32)
    local_pos = jnp.arange(date_dev, dtype=jnp.int32)
    slot_ids = jnp.arange(CAP, dtype=jnp.int32)
    looks_list = []
    for round_index in range(pairs.shape[0]):
        block = pairs[round_index]
        own_pairs = lax.dynamic_slice_in_dim(block, own_index * pair_dev, pair_dev, 0)
        entries = own_pairs.reshape(-1)
        wanted = block.reshape(date_count, 2 * pair_dev)
        needed = jnp.any(wanted[:, :, None] == local_ids[None, None, :], axis=1).astype(jnp.int32)
        ranks = jnp.cumsum(needed, axis=1) - needed
        picked = needed[:, None, :] * (ranks[:, None, :] == slot_ids[None, :, None]).astype(
            jnp.int32
        )
        source_local = jnp.sum(picked * local_pos[None, None, :], axis=2)
        present = jnp.sum(picked, axis=2) > 0
        outgoing = jnp.take(quantized, source_local.reshape(-1), axis=0).reshape(
            (date_count, CAP) + tile_shape
        )
        outgoing = jnp.where(present[:, :, None, None, None], outgoing, jnp.zeros((), jnp.bfloat16))
        incoming = lax.all_to_all(outgoing, "date", split_axis=0, concat_axis=0, tiled=True)
        matches = entries[:, None] == all_ids[None, :]
        my_need = jnp.any(matches, axis=0).astype(jnp.int32).reshape(date_count, date_dev)
        my_rank = (jnp.cumsum(my_need, axis=1) - my_need).reshape(-1)
        entry_slot = jnp.sum(jnp.where(matches, my_rank[None, :], 0), axis=1)
        position = entries // date_dev * CAP + entry_slot
        fetched = jnp.take(incoming.reshape((date_count * CAP,) + tile_shape), position, axis=0)
        looks = pair_looks(fetched.reshape((pair_dev, 2) + tile_shape))
        looks_list.append(looks)
    stacked = jnp.stack(looks_list, axis=0)
    padded = with_halo(stacked, (("az", 3),), 2)
    coherence = coherence_from(padded)
    interferogram = stacked[:, :, 0:2]
    return (interferogram, coherence)


LINES, SAMPLES = 4, 16
STEPS = ((0, 2, 2), (0, 2, 1), (1, 8, 8), (1, 8, 4), (1, 8, 2), (1, 8, 1))


def iota(shape, dim):
    return lax.broadcasted_iota(jnp.int32, shape, dim)


def place_of(leaf):
    bit = [(leaf >> n) & 1 for n in range(6)]
    return 32 * bit[3] + 16 * bit[4] + 8 * bit[5] + 4 * bit[0] + 2 * bit[1] + bit[2]


def rolled(x, shift, dim):
    return pltpu.roll(x, shift % x.shape[dim], dim)


def join(one, two, dim, unit, dist, phase):
    low = ((iota(one.shape, dim) - unit * phase) & (unit * dist)) == 0
    kept = jnp.where(low, one, two)
    other = jnp.where(low, two, one)
    return kept + rolled(other, -unit * dist, dim)


def cell_sums(real, imag):
    count = len(real)
    couples = [(i, j) for i in range(count) for j in range(i + 1, count)]

    def quantity(place):
        if place < len(couples):
            i, j = couples[place]
            return real[i] * real[j] + imag[i] * imag[j]
        place -= len(couples)
        if place < len(couples):
            i, j = couples[place]
            return imag[i] * real[j] - real[i] * imag[j]
        i = place - len(couples)
        return real[i] * real[i] + imag[i] * imag[i]

    def build(level, base, phases):
        if level == 0:
            return quantity(place_of(base))
        dim, unit, dist = STEPS[level - 1]
        moved = tuple(p + dist if d == dim else p for d, p in enumerate(phases))
        one = build(level - 1, base, phases)
        two = build(level - 1, base + (1 << (level - 1)), moved)
        return join(one, two, dim, unit, dist, phases[dim])

    return build(len(STEPS), 0, (0, 0))


def exact_dot(a, b):
    return lax.dot_general(
        a,
        b,
        (((1,), (0,)), ((), ())),
        precision=lax.Precision.HIGHEST,
        preferred_element_type=jnp.float32,
    )


def sample_order():
    src, dst = iota((128, 128), 0), iota((128, 128), 1)
    hit = dst == (src % SAMPLES) * (128 // SAMPLES) + src // SAMPLES
    return jnp.where(hit, 1.0 / 8, 0.0).astype(jnp.bfloat16)


def table_of(tiles):
    lane, sub = iota((8, 128), 1), iota((8, 128), 0)
    tiles = list(tiles)
    for b in range(3):
        dist = 8 << b
        low = (lane & dist) == 0
        for j in range(8):
            if not j >> b & 1:
                one, two = tiles[j], tiles[j | 1 << b]
                tiles[j] = jnp.where(low, one, rolled(two, dist, 1))
                tiles[j | 1 << b] = jnp.where(low, rolled(one, -dist, 1), two)
    even, first = (sub & 1) == 0, lane < 64
    out = []
    for tile in tiles:
        far = rolled(tile, 64, 1)
        moved = jnp.where(even, rolled(far, -1, 0), rolled(far, 1, 0))
        out.append(jnp.where(even == first, tile, moved))
    return out


def box_of(own, before, after):
    lane = iota(own.shape, 1)
    first = lane < 64
    both = own + rolled(own, 64, 1)
    both = both + jnp.where(first, before + rolled(before, 64, 1), before)
    both = both + jnp.where(first, after, after + rolled(after, 64, 1))
    cell = lane & 63
    out = both
    for o in (-2, -1, 1, 2):
        valid = (cell + o >= 0) & (cell + o < 64)
        out = out + jnp.where(valid, rolled(both, -o, 1), 0.0)
    return out


def pick(places, values):
    return jnp.where(iota((64, 128), 0) == places, values, 0.0)


def picks(rank_a, rank_b, count):
    first = iota(rank_a.shape, 1) < 64
    low, high = jnp.minimum(rank_a, rank_b), jnp.maximum(rank_a, rank_b)
    couples = count * (count - 1) // 2
    place = ((low * (2 * count - 1 - low)) >> 1) + high - low - 1
    sign = jnp.where(first | (rank_a < rank_b), 1.0, -1.0)
    products = pick(place + jnp.where(first, 0, couples), sign)
    powers = pick(2 * couples + jnp.where(first, rank_a, rank_b), jnp.ones_like(sign))
    return products, powers


MESH = pl.DeviceIdType.MESH


def list_dates(pairs, dates, peers):
    length = pairs.shape[1]
    part = length // peers
    date = iota((dates, length), 0)
    named = (pairs[0:1] == date) | (pairs[1:2] == date)
    parts = iota((length, 128), 0) // part == iota((length, 128), 1)
    dims = (((1,), (0,)), ((), ()))
    one = jnp.bfloat16
    counts = lax.dot_general(
        named.astype(jnp.float32).astype(one),
        parts.astype(jnp.float32).astype(one),
        dims,
        preferred_element_type=jnp.float32,
    )
    needed = counts > 0.5
    before = iota((dates, dates), 1) < iota((dates, dates), 0)
    rank = lax.dot_general(
        before.astype(jnp.float32).astype(one),
        needed.astype(jnp.float32).astype(one),
        dims,
        preferred_element_type=jnp.float32,
    )
    rank = jnp.where(needed, rank, -1.0).astype(jnp.int32)
    date = iota(rank.shape, 0)
    rows = [jnp.sum(jnp.where(rank == k, date, 0), axis=0, keepdims=True) for k in range(peers)]
    return jnp.concatenate(rows, 0)


def stack_kernel(
    slc_ref,
    pairs_ref,
    ifg_ref,
    coh_ref,
    lines,
    sent,
    held,
    full,
    sums,
    tiles,
    table,
    halo,
    listed,
    ids,
    line_sem,
    send_a,
    recv_a,
    send_b,
    recv_b,
    send_h,
    recv_h,
    list_sem,
):
    peers, az_size = lax.axis_size("date"), lax.axis_size("az")
    me, az = lax.axis_index("date"), lax.axis_index("az")
    date_dev = slc_ref.shape[0]
    rounds = pairs_ref.shape[0]
    width = slc_ref.shape[3] // peers
    images_dev = 2 * date_dev
    sides = ((-1, az > 0), (1, az < az_size - 1))

    barrier = pltpu.get_barrier_semaphore()
    for o in range(1, peers):
        pl.semaphore_signal(
            barrier, inc=1, device_id={"date": lax.rem(me + o, peers)}, device_id_type=MESH
        )
    for step, there in sides:

        @pl.when(there)
        def _():
            pl.semaphore_signal(barrier, inc=1, device_id={"az": az + step}, device_id_type=MESH)

    def line(n):
        row = n % LINES * 2 + n // LINES
        return pltpu.make_async_copy(
            slc_ref.at[:, :, n, :], lines.at[:, :, row, :], line_sem.at[n]
        )

    for n in range(2 * LINES):
        line(n).start()
    for n in range(2 * LINES):
        line(n).wait()
    for j in range(peers):
        part = lines[:, :, :, j * width : (j + 1) * width]
        sent[j] = part.reshape(sent.shape[1:]).astype(jnp.bfloat16)
    greeted = peers - 1 + (az > 0).astype(jnp.int32) + (az < az_size - 1).astype(jnp.int32)
    pl.semaphore_wait(barrier, greeted)

    def images(o):
        peer = lax.rem(me + o, peers)
        return pltpu.make_async_remote_copy(
            src_ref=sent.at[peer],
            dst_ref=held.at[me],
            send_sem=send_a.at[o],
            recv_sem=recv_a.at[o],
            device_id={"date": peer},
            device_id_type=MESH,
        )

    for o in range(1, peers):
        images(o).start()
    for r in range(rounds):
        listed[r * peers : (r + 1) * peers, :] = list_dates(
            pairs_ref[r], date_dev * peers, peers
        )
    fetch = pltpu.make_async_copy(listed, ids, list_sem)
    fetch.start()
    order = sample_order()

    def take(owner, block):
        spread = jnp.dot(block, order, preferred_element_type=jnp.float32)
        at = pl.ds(owner * images_dev, images_dev)
        full[at] = spread.reshape((images_dev,) + full.shape[1:])

    take(me, sent[me])
    fetch.wait()
    lane = iota((1, 128), 1)
    chosen = []
    for r in range(rounds):
        ranks = []
        for c in range(2):
            start = pl.multiple_of(me // 2 * 128, 128)
            near = pairs_ref[r, c : c + 1, pl.ds(start, 128)]
            own = jnp.where((lane < 64) == (lax.rem(me, 2) == 0), near, rolled(near, 64, 1))
            rank = jnp.zeros_like(own)
            for k in range(peers):
                rank = rank + (own > ids[r * peers + k, me]).astype(jnp.int32)
            ranks.append(rank)
        chosen.append(ranks)
    for o in range(1, peers):
        images(o).wait_recv()
        owner = lax.rem(me + peers - o, peers)
        take(owner, held[owner])

    def results(o):
        peer = lax.rem(me + o, peers)
        return pltpu.make_async_remote_copy(
            src_ref=sums.at[peer],
            dst_ref=tiles.at[me],
            send_sem=send_b.at[o],
            recv_sem=recv_b.at[o],
            device_id={"date": peer},
            device_id_type=MESH,
        )

    def serve(o, carry):
        peer = lax.rem(me + o, peers)
        for r in range(rounds):
            real, imag = [], []
            for k in range(peers):
                date = ids[r * peers + k, peer]
                real.append(full[2 * date])
                imag.append(full[2 * date + 1])
            sums[peer, r] = cell_sums(real, imag)

        @pl.when(o < peers)
        def _():
            results(o).start()

        return carry

    lax.fori_loop(1, peers + 1, serve, 0)
    tiles[me] = sums[me]
    for o in range(1, peers):
        results(o).wait_recv()
    for r in range(rounds):
        for k, tile in enumerate(table_of([tiles[j, r] for j in range(peers)])):
            table[r, 8 * k : 8 * k + 8, :] = tile

    def edge(n, step):
        return pltpu.make_async_remote_copy(
            src_ref=table,
            dst_ref=halo.at[n],
            send_sem=send_h.at[n],
            recv_sem=recv_h.at[n],
            device_id={"az": az + step},
            device_id_type=MESH,
        )

    for n, (step, there) in enumerate(sides):

        @pl.when(there)
        def _():
            edge(n, step).start()

        @pl.when(jnp.logical_not(there))
        def _():
            halo[1 - n] = jnp.zeros_like(halo[1 - n])

    matrices = []
    for r in range(rounds):
        products, powers = picks(*chosen[r], peers)
        products, powers = products.T, powers.T
        matrices.append((products, powers))
        means = exact_dot(products, table[r])
        for c in range(2):
            for row in range(2):
                ifg_ref[r, :, c, row, :] = means[64 * c : 64 * c + 64, 64 * row : 64 * row + 64]

    for n, (step, there) in enumerate(sides):

        @pl.when(there)
        def _():
            edge(1 - n, step).wait_recv()

    for r in range(rounds):
        products, powers = matrices[r]
        boxed = box_of(table[r], halo[1, r], halo[0, r])
        parts = exact_dot(products, boxed)
        power = exact_dot(powers, boxed)
        size = jnp.sqrt(parts[:64] * parts[:64] + parts[64:] * parts[64:])
        coherence = size / jnp.sqrt(power[:64] * power[64:])
        for row in range(2):
            coh_ref[r, :, row, :] = coherence[:, 64 * row : 64 * row + 64]

    for o in range(1, peers):
        images(o).wait_send()
        results(o).wait_send()
    for n, (step, there) in enumerate(sides):

        @pl.when(there)
        def _():
            edge(n, step).wait_send()


def per_device_few(slc, pairs):
    peers = lax.axis_size("date")
    rounds = pairs.shape[0]
    pair_dev = pairs.shape[1] // peers
    date_dev, _, lines, columns = slc.shape
    width = columns // peers
    rows = date_dev * 2 * lines
    cells = columns // SAMPLES
    vmem = pl.BlockSpec(memory_space=pltpu.VMEM)
    dma = pltpu.SemaphoreType.DMA
    return pl.pallas_call(
        stack_kernel,
        out_shape=(
            jax.ShapeDtypeStruct((rounds, pair_dev, 2, lines // LINES, cells), jnp.float32),
            jax.ShapeDtypeStruct((rounds, pair_dev, lines // LINES, cells), jnp.float32),
        ),
        in_specs=[pl.BlockSpec(memory_space=pl.ANY), vmem],
        out_specs=(vmem, vmem),
        scratch_shapes=[
            pltpu.VMEM(slc.shape, jnp.float32),
            pltpu.VMEM((peers, rows, width), jnp.bfloat16),
            pltpu.VMEM((peers, rows, width), jnp.bfloat16),
            pltpu.VMEM((peers * date_dev * 2, lines, width), jnp.float32),
            pltpu.VMEM((peers, rounds, 8, 128), jnp.float32),
            pltpu.VMEM((peers, rounds, 8, 128), jnp.float32),
            pltpu.VMEM((rounds, 64, 128), jnp.float32),
            pltpu.VMEM((2, rounds, 64, 128), jnp.float32),
            pltpu.VMEM((rounds * peers, 128), jnp.int32),
            pltpu.SMEM((rounds * peers, 128), jnp.int32),
            dma((lines,)),
            dma((peers,)),
            dma((peers,)),
            dma((peers,)),
            dma((peers,)),
            dma((2,)),
            dma((2,)),
            dma,
        ],
        compiler_params=pltpu.CompilerParams(collective_id=0, has_side_effects=True),
    )(slc, pairs.transpose(0, 2, 1))


def per_device(slc, pairs):
    peers = lax.axis_size("date")
    lines, columns = slc.shape[2:]
    pair_dev = pairs.shape[1] // peers
    few = (peers, pair_dev, lines, columns) == (8, 64, 2 * LINES, 64 * SAMPLES)
    return per_device_few(slc, pairs) if few else per_device_general(slc, pairs)


def solution(mesh):
    return jax.shard_map(
        per_device,
        mesh=mesh,
        in_specs=(P("date", None, "az", None), P()),
        out_specs=(P(None, "date", None, "az", None), P(None, "date", "az", None)),
        check_vma=False,
    )
```

```python
import jax
import jax.numpy as jnp
from jax import lax
from jax.experimental import pallas as pl
from jax.experimental.pallas import tpu as pltpu
from jax.sharding import PartitionSpec as P

CAP = 2


def with_halo(shard, sides, width):
    for axis, dim in sides:
        peers, length = (lax.axis_size(axis), shard.shape[dim])
        up = [(i, (i + 1) % peers) for i in range(peers - 1)]
        down = [(j, i) for i, j in up]
        last = lax.slice_in_dim(shard, length - width, length, axis=dim)
        first = lax.slice_in_dim(shard, 0, width, axis=dim)
        before = lax.ppermute(last, axis, up)
        after = lax.ppermute(first, axis, down)
        shard = jnp.concatenate([before, shard, after], axis=dim)
    return shard


def multilook(field):
    shape = field.shape
    blocks = field.reshape(shape[:-2] + (shape[-2] // 4, 4, shape[-1] // 16, 16))
    return blocks.mean(axis=(-3, -1))


def pair_looks(tiles):
    first = tiles[:, 0].astype(jnp.float32)
    second = tiles[:, 1].astype(jnp.float32)
    first_re, first_im = (first[:, 0], first[:, 1])
    second_re, second_im = (second[:, 0], second[:, 1])
    prod_re = first_re * second_re + first_im * second_im
    prod_im = first_im * second_re - first_re * second_im
    power_a = first_re * first_re + first_im * first_im
    power_b = second_re * second_re + second_im * second_im
    return jnp.stack(
        [multilook(prod_re), multilook(prod_im), multilook(power_a), multilook(power_b)], axis=1
    )


def coherence_from(padded):
    lines = padded.shape[-2] - 4
    columns = padded.shape[-1]
    az_sum = padded[..., 0:lines, :]
    for offset in range(1, 5):
        az_sum = az_sum + padded[..., offset : offset + lines, :]
    widths = [(0, 0)] * (az_sum.ndim - 1) + [(2, 2)]
    wide = jnp.pad(az_sum, widths)
    boxed = wide[..., 0:columns]
    for offset in range(1, 5):
        boxed = boxed + wide[..., offset : offset + columns]
    numer = jnp.sqrt(boxed[..., 0, :, :] ** 2 + boxed[..., 1, :, :] ** 2)
    return numer / jnp.sqrt(boxed[..., 2, :, :] * boxed[..., 3, :, :])


def per_device_general(slc, pairs):
    date_count = lax.axis_size("date")
    own_index = lax.axis_index("date")
    date_dev = slc.shape[0]
    pair_dev = pairs.shape[1] // date_count
    tile_shape = slc.shape[1:]
    quantized = lax.optimization_barrier(slc.astype(jnp.bfloat16))
    all_ids = jnp.arange(date_count * date_dev, dtype=jnp.int32)
    local_ids = own_index * date_dev + jnp.arange(date_dev, dtype=jnp.int32)
    local_pos = jnp.arange(date_dev, dtype=jnp.int32)
    slot_ids = jnp.arange(CAP, dtype=jnp.int32)
    looks_list = []
    for round_index in range(pairs.shape[0]):
        block = pairs[round_index]
        own_pairs = lax.dynamic_slice_in_dim(block, own_index * pair_dev, pair_dev, 0)
        entries = own_pairs.reshape(-1)
        wanted = block.reshape(date_count, 2 * pair_dev)
        needed = jnp.any(wanted[:, :, None] == local_ids[None, None, :], axis=1).astype(jnp.int32)
        ranks = jnp.cumsum(needed, axis=1) - needed
        picked = needed[:, None, :] * (ranks[:, None, :] == slot_ids[None, :, None]).astype(
            jnp.int32
        )
        source_local = jnp.sum(picked * local_pos[None, None, :], axis=2)
        present = jnp.sum(picked, axis=2) > 0
        outgoing = jnp.take(quantized, source_local.reshape(-1), axis=0).reshape(
            (date_count, CAP) + tile_shape
        )
        outgoing = jnp.where(present[:, :, None, None, None], outgoing, jnp.zeros((), jnp.bfloat16))
        incoming = lax.all_to_all(outgoing, "date", split_axis=0, concat_axis=0, tiled=True)
        matches = entries[:, None] == all_ids[None, :]
        my_need = jnp.any(matches, axis=0).astype(jnp.int32).reshape(date_count, date_dev)
        my_rank = (jnp.cumsum(my_need, axis=1) - my_need).reshape(-1)
        entry_slot = jnp.sum(jnp.where(matches, my_rank[None, :], 0), axis=1)
        position = entries // date_dev * CAP + entry_slot
        fetched = jnp.take(incoming.reshape((date_count * CAP,) + tile_shape), position, axis=0)
        looks = pair_looks(fetched.reshape((pair_dev, 2) + tile_shape))
        looks_list.append(looks)
    stacked = jnp.stack(looks_list, axis=0)
    padded = with_halo(stacked, (("az", 3),), 2)
    coherence = coherence_from(padded)
    interferogram = stacked[:, :, 0:2]
    return (interferogram, coherence)


LINES, SAMPLES = 4, 16
STEPS = ((0, 2, 2), (0, 2, 1), (1, 8, 8), (1, 8, 4), (1, 8, 2), (1, 8, 1))


def iota(shape, dim):
    return lax.broadcasted_iota(jnp.int32, shape, dim)


def place_of(leaf):
    bit = [(leaf >> n) & 1 for n in range(6)]
    return 32 * bit[3] + 16 * bit[4] + 8 * bit[5] + 4 * bit[0] + 2 * bit[1] + bit[2]


def rolled(x, shift, dim):
    return pltpu.roll(x, shift % x.shape[dim], dim)


def join(one, two, dim, unit, dist, phase):
    low = ((iota(one.shape, dim) - unit * phase) & (unit * dist)) == 0
    kept = jnp.where(low, one, two)
    other = jnp.where(low, two, one)
    return kept + rolled(other, -unit * dist, dim)


def cell_sums(real, imag):
    count = len(real)
    couples = [(i, j) for i in range(count) for j in range(i + 1, count)]

    def quantity(place):
        if place < len(couples):
            i, j = couples[place]
            return real[i] * real[j] + imag[i] * imag[j]
        place -= len(couples)
        if place < len(couples):
            i, j = couples[place]
            return imag[i] * real[j] - real[i] * imag[j]
        i = place - len(couples)
        return real[i] * real[i] + imag[i] * imag[i]

    def build(level, base, phases):
        if level == 0:
            return quantity(place_of(base))
        dim, unit, dist = STEPS[level - 1]
        moved = tuple(p + dist if d == dim else p for d, p in enumerate(phases))
        one = build(level - 1, base, phases)
        two = build(level - 1, base + (1 << (level - 1)), moved)
        return join(one, two, dim, unit, dist, phases[dim])

    return build(len(STEPS), 0, (0, 0))


def in_three(x):
    parts = []
    for _ in range(3):
        part = x.astype(jnp.bfloat16)
        parts.append(part)
        x = x - part.astype(jnp.float32)
    return jnp.concatenate(parts, 0)


def sample_order():
    src, dst = iota((128, 128), 0), iota((128, 128), 1)
    hit = dst == (src % SAMPLES) * (128 // SAMPLES) + src // SAMPLES
    return jnp.where(hit, 1.0 / 8, 0.0).astype(jnp.bfloat16)


def table_of(tiles):
    lane, sub = iota((8, 128), 1), iota((8, 128), 0)
    tiles = list(tiles)
    for b in range(3):
        dist = 8 << b
        low = (lane & dist) == 0
        for j in range(8):
            if not j >> b & 1:
                one, two = tiles[j], tiles[j | 1 << b]
                tiles[j] = jnp.where(low, one, rolled(two, dist, 1))
                tiles[j | 1 << b] = jnp.where(low, rolled(one, -dist, 1), two)
    even, first = (sub & 1) == 0, lane < 64
    out = []
    for tile in tiles:
        far = rolled(tile, 64, 1)
        moved = jnp.where(even, rolled(far, -1, 0), rolled(far, 1, 0))
        out.append(jnp.where(even == first, tile, moved))
    return out


def box_of(own, before, after):
    lane = iota(own.shape, 1)
    first = lane < 64
    both = own + rolled(own, 64, 1)
    both = both + jnp.where(first, before + rolled(before, 64, 1), before)
    both = both + jnp.where(first, after, after + rolled(after, 64, 1))
    cell = lane & 63
    out = both
    for o in (-2, -1, 1, 2):
        valid = (cell + o >= 0) & (cell + o < 64)
        out = out + jnp.where(valid, rolled(both, -o, 1), 0.0)
    return out


def pick(places, values):
    return jnp.where(iota((192, 128), 0) & 63 == places, values, 0.0)


def picks(rank_a, rank_b, count):
    first = iota(rank_a.shape, 1) < 64
    low, high = jnp.minimum(rank_a, rank_b), jnp.maximum(rank_a, rank_b)
    couples = count * (count - 1) // 2
    place = ((low * (2 * count - 1 - low)) >> 1) + high - low - 1
    sign = jnp.where(first | (rank_a < rank_b), 1.0, -1.0)
    products = pick(place + jnp.where(first, 0, couples), sign)
    powers = pick(2 * couples + jnp.where(first, rank_a, rank_b), jnp.ones_like(sign))
    return products, powers


MESH = pl.DeviceIdType.MESH


def list_dates(pairs, dates, peers):
    length = pairs.shape[1]
    part = length // peers
    date = iota((dates, length), 0)
    named = (pairs[0:1] == date) | (pairs[1:2] == date)
    parts = iota((length, 128), 0) // part == iota((length, 128), 1)
    dims = (((1,), (0,)), ((), ()))
    one = jnp.bfloat16
    counts = lax.dot_general(
        named.astype(jnp.float32).astype(one),
        parts.astype(jnp.float32).astype(one),
        dims,
        preferred_element_type=jnp.float32,
    )
    needed = counts > 0.5
    before = iota((dates, dates), 1) < iota((dates, dates), 0)
    rank = lax.dot_general(
        before.astype(jnp.float32).astype(one),
        needed.astype(jnp.float32).astype(one),
        dims,
        preferred_element_type=jnp.float32,
    )
    rank = jnp.where(needed, rank, -1.0).astype(jnp.int32)
    date = iota(rank.shape, 0)
    rows = [jnp.sum(jnp.where(rank == k, date, 0), axis=0, keepdims=True) for k in range(peers)]
    return jnp.concatenate(rows, 0)


def stack_kernel(
    slc_ref,
    pairs_ref,
    ifg_ref,
    coh_ref,
    lines,
    sent,
    held,
    full,
    sums,
    tiles,
    table,
    halo,
    chosen,
    listed,
    ids,
    line_sem,
    send_a,
    recv_a,
    send_b,
    recv_b,
    send_h,
    recv_h,
    list_sem,
):
    peers, az_size = lax.axis_size("date"), lax.axis_size("az")
    me, az = lax.axis_index("date"), lax.axis_index("az")
    date_dev = slc_ref.shape[0]
    rounds = pairs_ref.shape[0]
    width = slc_ref.shape[3] // peers
    images_dev = 2 * date_dev
    sides = ((-1, az > 0), (1, az < az_size - 1))

    barrier = pltpu.get_barrier_semaphore()
    for o in range(1, peers):
        pl.semaphore_signal(
            barrier, inc=1, device_id={"date": lax.rem(me + o, peers)}, device_id_type=MESH
        )
    for step, there in sides:

        @pl.when(there)
        def _():
            pl.semaphore_signal(barrier, inc=1, device_id={"az": az + step}, device_id_type=MESH)

    def line(n):
        row = n % LINES * 2 + n // LINES
        return pltpu.make_async_copy(
            slc_ref.at[:, :, n, :], lines.at[:, :, row, :], line_sem.at[n]
        )

    for n in range(2 * LINES):
        line(n).start()
    for n in range(2 * LINES):
        line(n).wait()
    for j in range(peers):
        part = lines[:, :, :, j * width : (j + 1) * width]
        sent[j] = part.reshape(sent.shape[1:]).astype(jnp.bfloat16)
    greeted = peers - 1 + (az > 0).astype(jnp.int32) + (az < az_size - 1).astype(jnp.int32)
    pl.semaphore_wait(barrier, greeted)

    def images(o):
        peer = lax.rem(me + o, peers)
        return pltpu.make_async_remote_copy(
            src_ref=sent.at[peer],
            dst_ref=held.at[me],
            send_sem=send_a.at[o],
            recv_sem=recv_a.at[o],
            device_id={"date": peer},
            device_id_type=MESH,
        )

    for o in range(1, peers):
        images(o).start()
    for r in range(rounds):
        listed[r * peers : (r + 1) * peers, :] = list_dates(
            pairs_ref[r], date_dev * peers, peers
        )
    fetch = pltpu.make_async_copy(listed, ids, list_sem)
    fetch.start()
    order = sample_order()

    def take(owner, block):
        spread = jnp.dot(block, order, preferred_element_type=jnp.float32)
        at = pl.ds(owner * images_dev, images_dev)
        full[at] = spread.reshape((images_dev,) + full.shape[1:])

    take(me, sent[me])
    fetch.wait()
    lane = iota((1, 128), 1)
    for r in range(rounds):
        ranks = []
        for c in range(2):
            start = pl.multiple_of(me // 2 * 128, 128)
            near = pairs_ref[r, c : c + 1, pl.ds(start, 128)]
            own = jnp.where((lane < 64) == (lax.rem(me, 2) == 0), near, rolled(near, 64, 1))
            rank = jnp.zeros_like(own)
            for k in range(peers):
                rank = rank + (own > ids[r * peers + k, me]).astype(jnp.int32)
            ranks.append(rank)
        products, powers = picks(*ranks, peers)
        chosen[r, :128, :] = products.T.astype(jnp.bfloat16)
        chosen[r, 128:, :] = powers.T.astype(jnp.bfloat16)
    for o in range(1, peers):
        images(o).wait_recv()
        owner = lax.rem(me + peers - o, peers)
        take(owner, held[owner])

    def results(o):
        peer = lax.rem(me + o, peers)
        return pltpu.make_async_remote_copy(
            src_ref=sums.at[peer],
            dst_ref=tiles.at[me],
            send_sem=send_b.at[o],
            recv_sem=recv_b.at[o],
            device_id={"date": peer},
            device_id_type=MESH,
        )

    def serve(o, carry):
        peer = lax.rem(me + o, peers)
        for r in range(rounds):
            real, imag = [], []
            for k in range(peers):
                date = ids[r * peers + k, peer]
                real.append(full[2 * date])
                imag.append(full[2 * date + 1])
            sums[peer, r] = cell_sums(real, imag)

        @pl.when(o < peers)
        def _():
            results(o).start()

        return carry

    lax.fori_loop(1, peers + 1, serve, 0)
    tiles[me] = sums[me]
    for o in range(1, peers):
        results(o).wait_recv()
    for r in range(rounds):
        for k, tile in enumerate(table_of([tiles[j, r] for j in range(peers)])):
            table[r, 8 * k : 8 * k + 8, :] = tile

    def edge(n, step):
        return pltpu.make_async_remote_copy(
            src_ref=table,
            dst_ref=halo.at[n],
            send_sem=send_h.at[n],
            recv_sem=recv_h.at[n],
            device_id={"az": az + step},
            device_id_type=MESH,
        )

    for n, (step, there) in enumerate(sides):

        @pl.when(there)
        def _():
            edge(n, step).start()

        @pl.when(jnp.logical_not(there))
        def _():
            halo[1 - n] = jnp.zeros_like(halo[1 - n])

    for r in range(rounds):
        means = jnp.dot(
            chosen[r, :128, :], in_three(table[r]), preferred_element_type=jnp.float32
        )
        for c in range(2):
            for row in range(2):
                ifg_ref[pl.ds(256 * r + 2 * c + row, 64, stride=4), :] = means[64 * c : 64 * c + 64, 64 * row : 64 * row + 64]

    for n, (step, there) in enumerate(sides):

        @pl.when(there)
        def _():
            edge(1 - n, step).wait_recv()

    for r in range(rounds):
        boxed = box_of(table[r], halo[1, r], halo[0, r])
        parts = jnp.dot(chosen[r], in_three(boxed), preferred_element_type=jnp.float32)
        size = jnp.sqrt(parts[:64] * parts[:64] + parts[64:128] * parts[64:128])
        coherence = size / jnp.sqrt(parts[128:192] * parts[192:])
        for row in range(2):
            coh_ref[pl.ds(128 * r + row, 64, stride=2), :] = coherence[:, 64 * row : 64 * row + 64]

    for o in range(1, peers):
        images(o).wait_send()
        results(o).wait_send()
    for n, (step, there) in enumerate(sides):

        @pl.when(there)
        def _():
            edge(n, step).wait_send()


def per_device_few(slc, pairs):
    peers = lax.axis_size("date")
    rounds = pairs.shape[0]
    pair_dev = pairs.shape[1] // peers
    date_dev, _, lines, columns = slc.shape
    width = columns // peers
    rows = date_dev * 2 * lines
    cells = columns // SAMPLES
    vmem = pl.BlockSpec(memory_space=pltpu.VMEM)
    dma = pltpu.SemaphoreType.DMA
    ifg, coh = pl.pallas_call(
        stack_kernel,
        out_shape=(
            jax.ShapeDtypeStruct((rounds * pair_dev * 2 * lines // LINES, cells), jnp.float32),
            jax.ShapeDtypeStruct((rounds * pair_dev * lines // LINES, cells), jnp.float32),
        ),
        in_specs=[pl.BlockSpec(memory_space=pl.ANY), vmem],
        out_specs=(vmem, vmem),
        scratch_shapes=[
            pltpu.VMEM(slc.shape, jnp.float32),
            pltpu.VMEM((peers, rows, width), jnp.bfloat16),
            pltpu.VMEM((peers, rows, width), jnp.bfloat16),
            pltpu.VMEM((peers * date_dev * 2, lines, width), jnp.float32),
            pltpu.VMEM((peers, rounds, 8, 128), jnp.float32),
            pltpu.VMEM((peers, rounds, 8, 128), jnp.float32),
            pltpu.VMEM((rounds, 64, 128), jnp.float32),
            pltpu.VMEM((2, rounds, 64, 128), jnp.float32),
            pltpu.VMEM((rounds, 256, 192), jnp.bfloat16),
            pltpu.VMEM((rounds * peers, 128), jnp.int32),
            pltpu.SMEM((rounds * peers, 128), jnp.int32),
            dma((lines,)),
            dma((peers,)),
            dma((peers,)),
            dma((peers,)),
            dma((peers,)),
            dma((2,)),
            dma((2,)),
            dma,
        ],
        compiler_params=pltpu.CompilerParams(collective_id=0, has_side_effects=True),
    )(slc, pairs.transpose(0, 2, 1))
    return (
        ifg.reshape(rounds, pair_dev, 2, lines // LINES, cells),
        coh.reshape(rounds, pair_dev, lines // LINES, cells),
    )


def per_device(slc, pairs):
    peers = lax.axis_size("date")
    lines, columns = slc.shape[2:]
    pair_dev = pairs.shape[1] // peers
    few = (peers, pair_dev, lines, columns) == (8, 64, 2 * LINES, 64 * SAMPLES)
    return per_device_few(slc, pairs) if few else per_device_general(slc, pairs)


def solution(mesh):
    return jax.shard_map(
        per_device,
        mesh=mesh,
        in_specs=(P("date", None, "az", None), P()),
        out_specs=(P(None, "date", None, "az", None), P(None, "date", "az", None)),
        check_vma=False,
    )
```

```python
import jax
import jax.numpy as jnp
from jax import lax
from jax.experimental import pallas as pl
from jax.experimental.pallas import tpu as pltpu
from jax.sharding import PartitionSpec as P

CAP = 2


def with_halo(shard, sides, width):
    for axis, dim in sides:
        peers, length = (lax.axis_size(axis), shard.shape[dim])
        up = [(i, (i + 1) % peers) for i in range(peers - 1)]
        down = [(j, i) for i, j in up]
        last = lax.slice_in_dim(shard, length - width, length, axis=dim)
        first = lax.slice_in_dim(shard, 0, width, axis=dim)
        before = lax.ppermute(last, axis, up)
        after = lax.ppermute(first, axis, down)
        shard = jnp.concatenate([before, shard, after], axis=dim)
    return shard


def multilook(field):
    shape = field.shape
    blocks = field.reshape(shape[:-2] + (shape[-2] // 4, 4, shape[-1] // 16, 16))
    return blocks.mean(axis=(-3, -1))


def pair_looks(tiles):
    first = tiles[:, 0].astype(jnp.float32)
    second = tiles[:, 1].astype(jnp.float32)
    first_re, first_im = (first[:, 0], first[:, 1])
    second_re, second_im = (second[:, 0], second[:, 1])
    prod_re = first_re * second_re + first_im * second_im
    prod_im = first_im * second_re - first_re * second_im
    power_a = first_re * first_re + first_im * first_im
    power_b = second_re * second_re + second_im * second_im
    return jnp.stack(
        [multilook(prod_re), multilook(prod_im), multilook(power_a), multilook(power_b)], axis=1
    )


def coherence_from(padded):
    lines = padded.shape[-2] - 4
    columns = padded.shape[-1]
    az_sum = padded[..., 0:lines, :]
    for offset in range(1, 5):
        az_sum = az_sum + padded[..., offset : offset + lines, :]
    widths = [(0, 0)] * (az_sum.ndim - 1) + [(2, 2)]
    wide = jnp.pad(az_sum, widths)
    boxed = wide[..., 0:columns]
    for offset in range(1, 5):
        boxed = boxed + wide[..., offset : offset + columns]
    numer = jnp.sqrt(boxed[..., 0, :, :] ** 2 + boxed[..., 1, :, :] ** 2)
    return numer / jnp.sqrt(boxed[..., 2, :, :] * boxed[..., 3, :, :])


def per_device_general(slc, pairs):
    date_count = lax.axis_size("date")
    own_index = lax.axis_index("date")
    date_dev = slc.shape[0]
    pair_dev = pairs.shape[1] // date_count
    tile_shape = slc.shape[1:]
    quantized = lax.optimization_barrier(slc.astype(jnp.bfloat16))
    all_ids = jnp.arange(date_count * date_dev, dtype=jnp.int32)
    local_ids = own_index * date_dev + jnp.arange(date_dev, dtype=jnp.int32)
    local_pos = jnp.arange(date_dev, dtype=jnp.int32)
    slot_ids = jnp.arange(CAP, dtype=jnp.int32)
    looks_list = []
    for round_index in range(pairs.shape[0]):
        block = pairs[round_index]
        own_pairs = lax.dynamic_slice_in_dim(block, own_index * pair_dev, pair_dev, 0)
        entries = own_pairs.reshape(-1)
        wanted = block.reshape(date_count, 2 * pair_dev)
        needed = jnp.any(wanted[:, :, None] == local_ids[None, None, :], axis=1).astype(jnp.int32)
        ranks = jnp.cumsum(needed, axis=1) - needed
        picked = needed[:, None, :] * (ranks[:, None, :] == slot_ids[None, :, None]).astype(
            jnp.int32
        )
        source_local = jnp.sum(picked * local_pos[None, None, :], axis=2)
        present = jnp.sum(picked, axis=2) > 0
        outgoing = jnp.take(quantized, source_local.reshape(-1), axis=0).reshape(
            (date_count, CAP) + tile_shape
        )
        outgoing = jnp.where(present[:, :, None, None, None], outgoing, jnp.zeros((), jnp.bfloat16))
        incoming = lax.all_to_all(outgoing, "date", split_axis=0, concat_axis=0, tiled=True)
        matches = entries[:, None] == all_ids[None, :]
        my_need = jnp.any(matches, axis=0).astype(jnp.int32).reshape(date_count, date_dev)
        my_rank = (jnp.cumsum(my_need, axis=1) - my_need).reshape(-1)
        entry_slot = jnp.sum(jnp.where(matches, my_rank[None, :], 0), axis=1)
        position = entries // date_dev * CAP + entry_slot
        fetched = jnp.take(incoming.reshape((date_count * CAP,) + tile_shape), position, axis=0)
        looks = pair_looks(fetched.reshape((pair_dev, 2) + tile_shape))
        looks_list.append(looks)
    stacked = jnp.stack(looks_list, axis=0)
    padded = with_halo(stacked, (("az", 3),), 2)
    coherence = coherence_from(padded)
    interferogram = stacked[:, :, 0:2]
    return (interferogram, coherence)


LINES, SAMPLES = 4, 16
STEPS = ((0, 2, 2), (0, 2, 1), (1, 8, 8), (1, 8, 4), (1, 8, 2), (1, 8, 1))


def iota(shape, dim):
    return lax.broadcasted_iota(jnp.int32, shape, dim)


def place_of(leaf):
    bit = [(leaf >> n) & 1 for n in range(6)]
    return 32 * bit[3] + 16 * bit[4] + 8 * bit[5] + 4 * bit[0] + 2 * bit[1] + bit[2]


def rolled(x, shift, dim):
    return pltpu.roll(x, shift % x.shape[dim], dim)


def join(one, two, dim, unit, dist, phase):
    low = ((iota(one.shape, dim) - unit * phase) & (unit * dist)) == 0
    kept = jnp.where(low, one, two)
    other = jnp.where(low, two, one)
    return kept + rolled(other, -unit * dist, dim)


def cell_sums(real, imag):
    count = len(real)
    couples = [(i, j) for i in range(count) for j in range(i + 1, count)]

    def quantity(place):
        if place < len(couples):
            i, j = couples[place]
            return real[i] * real[j] + imag[i] * imag[j]
        place -= len(couples)
        if place < len(couples):
            i, j = couples[place]
            return imag[i] * real[j] - real[i] * imag[j]
        i = place - len(couples)
        return real[i] * real[i] + imag[i] * imag[i]

    def build(level, base, phases):
        if level == 0:
            return quantity(place_of(base))
        dim, unit, dist = STEPS[level - 1]
        moved = tuple(p + dist if d == dim else p for d, p in enumerate(phases))
        one = build(level - 1, base, phases)
        two = build(level - 1, base + (1 << (level - 1)), moved)
        return join(one, two, dim, unit, dist, phases[dim])

    return build(len(STEPS), 0, (0, 0))


def in_three(x):
    parts = []
    for _ in range(3):
        part = x.astype(jnp.bfloat16)
        parts.append(part)
        x = x - part.astype(jnp.float32)
    return jnp.concatenate(parts, 0)


def sample_order():
    src, dst = iota((128, 128), 0), iota((128, 128), 1)
    hit = dst == (src % SAMPLES) * (128 // SAMPLES) + src // SAMPLES
    return jnp.where(hit, 1.0 / 8, 0.0).astype(jnp.bfloat16)


def table_of(tiles):
    lane, sub = iota((8, 128), 1), iota((8, 128), 0)
    tiles = list(tiles)
    for b in range(3):
        dist = 8 << b
        low = (lane & dist) == 0
        for j in range(8):
            if not j >> b & 1:
                one, two = tiles[j], tiles[j | 1 << b]
                tiles[j] = jnp.where(low, one, rolled(two, dist, 1))
                tiles[j | 1 << b] = jnp.where(low, rolled(one, -dist, 1), two)
    even, first = (sub & 1) == 0, lane < 64
    out = []
    for tile in tiles:
        far = rolled(tile, 64, 1)
        moved = jnp.where(even, rolled(far, -1, 0), rolled(far, 1, 0))
        out.append(jnp.where(even == first, tile, moved))
    return out


def box_of(own, before, after):
    lane = iota(own.shape, 1)
    first = lane < 64
    both = own + rolled(own, 64, 1)
    both = both + jnp.where(first, before + rolled(before, 64, 1), before)
    both = both + jnp.where(first, after, after + rolled(after, 64, 1))
    cell = lane & 63
    out = both
    for o in (-2, -1, 1, 2):
        valid = (cell + o >= 0) & (cell + o < 64)
        out = out + jnp.where(valid, rolled(both, -o, 1), 0.0)
    return out


def pick(places, values):
    return jnp.where(iota((192, 128), 0) & 63 == places, values, 0.0)


def picks(rank_a, rank_b, count):
    first = iota(rank_a.shape, 1) < 64
    low, high = jnp.minimum(rank_a, rank_b), jnp.maximum(rank_a, rank_b)
    couples = count * (count - 1) // 2
    place = ((low * (2 * count - 1 - low)) >> 1) + high - low - 1
    sign = jnp.where(first | (rank_a < rank_b), 1.0, -1.0)
    products = pick(place + jnp.where(first, 0, couples), sign)
    powers = pick(2 * couples + jnp.where(first, rank_a, rank_b), jnp.ones_like(sign))
    return products, powers


MESH = pl.DeviceIdType.MESH


def list_dates(pairs, dates, peers):
    length = pairs.shape[1]
    part = length // peers
    date = iota((dates, length), 0)
    named = (pairs[0:1] == date) | (pairs[1:2] == date)
    parts = iota((length, 128), 0) // part == iota((length, 128), 1)
    dims = (((1,), (0,)), ((), ()))
    one = jnp.bfloat16
    counts = lax.dot_general(
        named.astype(jnp.float32).astype(one),
        parts.astype(jnp.float32).astype(one),
        dims,
        preferred_element_type=jnp.float32,
    )
    needed = counts > 0.5
    before = iota((dates, dates), 1) < iota((dates, dates), 0)
    rank = lax.dot_general(
        before.astype(jnp.float32).astype(one),
        needed.astype(jnp.float32).astype(one),
        dims,
        preferred_element_type=jnp.float32,
    )
    rank = jnp.where(needed, rank, -1.0).astype(jnp.int32)
    date = iota(rank.shape, 0)
    rows = [jnp.sum(jnp.where(rank == k, date, 0), axis=0, keepdims=True) for k in range(peers)]
    return jnp.concatenate(rows, 0)


def stack_kernel(
    slc_ref,
    pairs_ref,
    table,
    boxed_ref,
    chosen,
    lines,
    sent,
    held,
    full,
    sums,
    tiles,
    halo,
    listed,
    ids,
    line_sem,
    send_a,
    recv_a,
    send_b,
    recv_b,
    send_h,
    recv_h,
    list_sem,
):
    peers, az_size = lax.axis_size("date"), lax.axis_size("az")
    me, az = lax.axis_index("date"), lax.axis_index("az")
    date_dev = slc_ref.shape[0]
    rounds = pairs_ref.shape[0]
    width = slc_ref.shape[3] // peers
    images_dev = 2 * date_dev
    sides = ((-1, az > 0), (1, az < az_size - 1))

    barrier = pltpu.get_barrier_semaphore()
    for o in range(1, peers):
        pl.semaphore_signal(
            barrier, inc=1, device_id={"date": lax.rem(me + o, peers)}, device_id_type=MESH
        )
    for step, there in sides:

        @pl.when(there)
        def _():
            pl.semaphore_signal(barrier, inc=1, device_id={"az": az + step}, device_id_type=MESH)

    def line(n):
        row = n % LINES * 2 + n // LINES
        return pltpu.make_async_copy(
            slc_ref.at[:, :, n, :], lines.at[:, :, row, :], line_sem.at[n]
        )

    for n in range(2 * LINES):
        line(n).start()
    for n in range(2 * LINES):
        line(n).wait()
    for j in range(peers):
        part = lines[:, :, :, j * width : (j + 1) * width]
        sent[j] = part.reshape(sent.shape[1:]).astype(jnp.bfloat16)
    greeted = peers - 1 + (az > 0).astype(jnp.int32) + (az < az_size - 1).astype(jnp.int32)
    pl.semaphore_wait(barrier, greeted)

    def images(o):
        peer = lax.rem(me + o, peers)
        return pltpu.make_async_remote_copy(
            src_ref=sent.at[peer],
            dst_ref=held.at[me],
            send_sem=send_a.at[o],
            recv_sem=recv_a.at[o],
            device_id={"date": peer},
            device_id_type=MESH,
        )

    for o in range(1, peers):
        images(o).start()
    for r in range(rounds):
        listed[r * peers : (r + 1) * peers, :] = list_dates(
            pairs_ref[r], date_dev * peers, peers
        )
    fetch = pltpu.make_async_copy(listed, ids, list_sem)
    fetch.start()
    order = sample_order()

    def take(owner, block):
        spread = jnp.dot(block, order, preferred_element_type=jnp.float32)
        at = pl.ds(owner * images_dev, images_dev)
        full[at] = spread.reshape((images_dev,) + full.shape[1:])

    take(me, sent[me])
    fetch.wait()
    lane = iota((1, 128), 1)
    for r in range(rounds):
        ranks = []
        for c in range(2):
            start = pl.multiple_of(me // 2 * 128, 128)
            near = pairs_ref[r, c : c + 1, pl.ds(start, 128)]
            own = jnp.where((lane < 64) == (lax.rem(me, 2) == 0), near, rolled(near, 64, 1))
            rank = jnp.zeros_like(own)
            for k in range(peers):
                rank = rank + (own > ids[r * peers + k, me]).astype(jnp.int32)
            ranks.append(rank)
        products, powers = picks(*ranks, peers)
        chosen[r, :128, :] = products.T.astype(jnp.bfloat16)
        chosen[r, 128:, :] = powers.T.astype(jnp.bfloat16)
    for o in range(1, peers):
        images(o).wait_recv()
        owner = lax.rem(me + peers - o, peers)
        take(owner, held[owner])

    def results(o):
        peer = lax.rem(me + o, peers)
        return pltpu.make_async_remote_copy(
            src_ref=sums.at[peer],
            dst_ref=tiles.at[me],
            send_sem=send_b.at[o],
            recv_sem=recv_b.at[o],
            device_id={"date": peer},
            device_id_type=MESH,
        )

    def serve(o, carry):
        peer = lax.rem(me + o, peers)
        for r in range(rounds):
            real, imag = [], []
            for k in range(peers):
                date = ids[r * peers + k, peer]
                real.append(full[2 * date])
                imag.append(full[2 * date + 1])
            sums[peer, r] = cell_sums(real, imag)

        @pl.when(o < peers)
        def _():
            results(o).start()

        return carry

    lax.fori_loop(1, peers + 1, serve, 0)
    tiles[me] = sums[me]
    for o in range(1, peers):
        results(o).wait_recv()
    for r in range(rounds):
        for k, tile in enumerate(table_of([tiles[j, r] for j in range(peers)])):
            table[r, 8 * k : 8 * k + 8, :] = tile

    def edge(n, step):
        return pltpu.make_async_remote_copy(
            src_ref=table,
            dst_ref=halo.at[n],
            send_sem=send_h.at[n],
            recv_sem=recv_h.at[n],
            device_id={"az": az + step},
            device_id_type=MESH,
        )

    for n, (step, there) in enumerate(sides):

        @pl.when(there)
        def _():
            edge(n, step).start()

        @pl.when(jnp.logical_not(there))
        def _():
            halo[1 - n] = jnp.zeros_like(halo[1 - n])

    for n, (step, there) in enumerate(sides):

        @pl.when(there)
        def _():
            edge(1 - n, step).wait_recv()

    for r in range(rounds):
        boxed_ref[r] = box_of(table[r], halo[1, r], halo[0, r])

    for o in range(1, peers):
        images(o).wait_send()
        results(o).wait_send()
    for n, (step, there) in enumerate(sides):

        @pl.when(there)
        def _():
            edge(n, step).wait_send()


def pairs_kernel(table_ref, boxed_ref, chosen_ref, ifg_ref, coh_ref):
    for r in range(table_ref.shape[0]):
        means = jnp.dot(
            chosen_ref[r, :128, :], in_three(table_ref[r]), preferred_element_type=jnp.float32
        )
        for c in range(2):
            for row in range(2):
                part = means[64 * c : 64 * c + 64, 64 * row : 64 * row + 64]
                ifg_ref[pl.ds(256 * r + 2 * c + row, 64, stride=4), :] = part
        parts = jnp.dot(
            chosen_ref[r], in_three(boxed_ref[r]), preferred_element_type=jnp.float32
        )
        size = jnp.sqrt(parts[:64] * parts[:64] + parts[64:128] * parts[64:128])
        coherence = size / jnp.sqrt(parts[128:192] * parts[192:])
        for row in range(2):
            part = coherence[:, 64 * row : 64 * row + 64]
            coh_ref[pl.ds(128 * r + row, 64, stride=2), :] = part


def per_device_few(slc, pairs):
    peers = lax.axis_size("date")
    rounds = pairs.shape[0]
    pair_dev = pairs.shape[1] // peers
    date_dev, _, lines, columns = slc.shape
    width = columns // peers
    rows = date_dev * 2 * lines
    cells = columns // SAMPLES
    vmem = pl.BlockSpec(memory_space=pltpu.VMEM)
    dma = pltpu.SemaphoreType.DMA
    found = pl.pallas_call(
        stack_kernel,
        out_shape=(
            jax.ShapeDtypeStruct((rounds, 64, 128), jnp.float32),
            jax.ShapeDtypeStruct((rounds, 64, 128), jnp.float32),
            jax.ShapeDtypeStruct((rounds, 256, 192), jnp.bfloat16),
        ),
        in_specs=[pl.BlockSpec(memory_space=pl.ANY), vmem],
        out_specs=(vmem,) * 3,
        scratch_shapes=[
            pltpu.VMEM(slc.shape, jnp.float32),
            pltpu.VMEM((peers, rows, width), jnp.bfloat16),
            pltpu.VMEM((peers, rows, width), jnp.bfloat16),
            pltpu.VMEM((peers * date_dev * 2, lines, width), jnp.float32),
            pltpu.VMEM((peers, rounds, 8, 128), jnp.float32),
            pltpu.VMEM((peers, rounds, 8, 128), jnp.float32),
            pltpu.VMEM((2, rounds, 64, 128), jnp.float32),
            pltpu.VMEM((rounds * peers, 128), jnp.int32),
            pltpu.SMEM((rounds * peers, 128), jnp.int32),
            dma((lines,)),
            dma((peers,)),
            dma((peers,)),
            dma((peers,)),
            dma((peers,)),
            dma((2,)),
            dma((2,)),
            dma,
        ],
        compiler_params=pltpu.CompilerParams(collective_id=0, has_side_effects=True),
    )(slc, pairs.transpose(0, 2, 1))
    ifg, coh = pl.pallas_call(
        pairs_kernel,
        out_shape=(
            jax.ShapeDtypeStruct((rounds * pair_dev * 2 * lines // LINES, cells), jnp.float32),
            jax.ShapeDtypeStruct((rounds * pair_dev * lines // LINES, cells), jnp.float32),
        ),
        in_specs=[vmem] * 3,
        out_specs=(vmem, vmem),
    )(*found)
    return (
        ifg.reshape(rounds, pair_dev, 2, lines // LINES, cells),
        coh.reshape(rounds, pair_dev, lines // LINES, cells),
    )


def per_device(slc, pairs):
    peers = lax.axis_size("date")
    lines, columns = slc.shape[2:]
    pair_dev = pairs.shape[1] // peers
    few = (peers, pair_dev, lines, columns) == (8, 64, 2 * LINES, 64 * SAMPLES)
    return per_device_few(slc, pairs) if few else per_device_general(slc, pairs)


def solution(mesh):
    return jax.shard_map(
        per_device,
        mesh=mesh,
        in_specs=(P("date", None, "az", None), P()),
        out_specs=(P(None, "date", None, "az", None), P(None, "date", "az", None)),
        check_vma=False,
    )
```

```python
import functools
import jax
import jax.numpy as jnp
from jax import lax
from jax.experimental import pallas as pl
from jax.experimental.pallas import tpu as pltpu
from jax.sharding import PartitionSpec as P

CAP = 2


def with_halo(shard, sides, width):
    for axis, dim in sides:
        peers, length = (lax.axis_size(axis), shard.shape[dim])
        up = [(i, (i + 1) % peers) for i in range(peers - 1)]
        down = [(j, i) for i, j in up]
        last = lax.slice_in_dim(shard, length - width, length, axis=dim)
        first = lax.slice_in_dim(shard, 0, width, axis=dim)
        before = lax.ppermute(last, axis, up)
        after = lax.ppermute(first, axis, down)
        shard = jnp.concatenate([before, shard, after], axis=dim)
    return shard


def multilook(field):
    shape = field.shape
    blocks = field.reshape(shape[:-2] + (shape[-2] // 4, 4, shape[-1] // 16, 16))
    return blocks.mean(axis=(-3, -1))


def pair_looks(tiles):
    first = tiles[:, 0].astype(jnp.float32)
    second = tiles[:, 1].astype(jnp.float32)
    first_re, first_im = (first[:, 0], first[:, 1])
    second_re, second_im = (second[:, 0], second[:, 1])
    prod_re = first_re * second_re + first_im * second_im
    prod_im = first_im * second_re - first_re * second_im
    power_a = first_re * first_re + first_im * first_im
    power_b = second_re * second_re + second_im * second_im
    return jnp.stack(
        [multilook(prod_re), multilook(prod_im), multilook(power_a), multilook(power_b)], axis=1
    )


def coherence_from(padded):
    lines = padded.shape[-2] - 4
    columns = padded.shape[-1]
    az_sum = padded[..., 0:lines, :]
    for offset in range(1, 5):
        az_sum = az_sum + padded[..., offset : offset + lines, :]
    widths = [(0, 0)] * (az_sum.ndim - 1) + [(2, 2)]
    wide = jnp.pad(az_sum, widths)
    boxed = wide[..., 0:columns]
    for offset in range(1, 5):
        boxed = boxed + wide[..., offset : offset + columns]
    numer = jnp.sqrt(boxed[..., 0, :, :] ** 2 + boxed[..., 1, :, :] ** 2)
    return numer / jnp.sqrt(boxed[..., 2, :, :] * boxed[..., 3, :, :])


def per_device_general(slc, pairs):
    date_count = lax.axis_size("date")
    own_index = lax.axis_index("date")
    date_dev = slc.shape[0]
    pair_dev = pairs.shape[1] // date_count
    tile_shape = slc.shape[1:]
    quantized = lax.optimization_barrier(slc.astype(jnp.bfloat16))
    all_ids = jnp.arange(date_count * date_dev, dtype=jnp.int32)
    local_ids = own_index * date_dev + jnp.arange(date_dev, dtype=jnp.int32)
    local_pos = jnp.arange(date_dev, dtype=jnp.int32)
    slot_ids = jnp.arange(CAP, dtype=jnp.int32)
    looks_list = []
    for round_index in range(pairs.shape[0]):
        block = pairs[round_index]
        own_pairs = lax.dynamic_slice_in_dim(block, own_index * pair_dev, pair_dev, 0)
        entries = own_pairs.reshape(-1)
        wanted = block.reshape(date_count, 2 * pair_dev)
        needed = jnp.any(wanted[:, :, None] == local_ids[None, None, :], axis=1).astype(jnp.int32)
        ranks = jnp.cumsum(needed, axis=1) - needed
        picked = needed[:, None, :] * (ranks[:, None, :] == slot_ids[None, :, None]).astype(
            jnp.int32
        )
        source_local = jnp.sum(picked * local_pos[None, None, :], axis=2)
        present = jnp.sum(picked, axis=2) > 0
        outgoing = jnp.take(quantized, source_local.reshape(-1), axis=0).reshape(
            (date_count, CAP) + tile_shape
        )
        outgoing = jnp.where(present[:, :, None, None, None], outgoing, jnp.zeros((), jnp.bfloat16))
        incoming = lax.all_to_all(outgoing, "date", split_axis=0, concat_axis=0, tiled=True)
        matches = entries[:, None] == all_ids[None, :]
        my_need = jnp.any(matches, axis=0).astype(jnp.int32).reshape(date_count, date_dev)
        my_rank = (jnp.cumsum(my_need, axis=1) - my_need).reshape(-1)
        entry_slot = jnp.sum(jnp.where(matches, my_rank[None, :], 0), axis=1)
        position = entries // date_dev * CAP + entry_slot
        fetched = jnp.take(incoming.reshape((date_count * CAP,) + tile_shape), position, axis=0)
        looks = pair_looks(fetched.reshape((pair_dev, 2) + tile_shape))
        looks_list.append(looks)
    stacked = jnp.stack(looks_list, axis=0)
    padded = with_halo(stacked, (("az", 3),), 2)
    coherence = coherence_from(padded)
    interferogram = stacked[:, :, 0:2]
    return (interferogram, coherence)


LINES, SAMPLES = 4, 16
STEPS = ((0, 2, 2), (0, 2, 1), (1, 8, 8), (1, 8, 4), (1, 8, 2), (1, 8, 1))


def iota(shape, dim):
    return lax.broadcasted_iota(jnp.int32, shape, dim)


def place_of(leaf):
    bit = [(leaf >> n) & 1 for n in range(6)]
    return 32 * bit[3] + 16 * bit[4] + 8 * bit[5] + 4 * bit[0] + 2 * bit[1] + bit[2]


def rolled(x, shift, dim):
    return pltpu.roll(x, shift % x.shape[dim], dim)


def join(one, two, dim, unit, dist, phase):
    low = ((iota(one.shape, dim) - unit * phase) & (unit * dist)) == 0
    kept = jnp.where(low, one, two)
    other = jnp.where(low, two, one)
    return kept + rolled(other, -unit * dist, dim)


def cell_sums(real, imag):
    count = len(real)
    couples = [(i, j) for i in range(count) for j in range(i + 1, count)]

    def quantity(place):
        if place < len(couples):
            i, j = couples[place]
            return real[i] * real[j] + imag[i] * imag[j]
        place -= len(couples)
        if place < len(couples):
            i, j = couples[place]
            return imag[i] * real[j] - real[i] * imag[j]
        i = place - len(couples)
        return real[i] * real[i] + imag[i] * imag[i]

    def build(level, base, phases):
        if level == 0:
            return quantity(place_of(base))
        dim, unit, dist = STEPS[level - 1]
        moved = tuple(p + dist if d == dim else p for d, p in enumerate(phases))
        one = build(level - 1, base, phases)
        two = build(level - 1, base + (1 << (level - 1)), moved)
        return join(one, two, dim, unit, dist, phases[dim])

    return build(len(STEPS), 0, (0, 0))


def in_three(x):
    parts = []
    for _ in range(3):
        part = x.astype(jnp.bfloat16)
        parts.append(part)
        x = x - part.astype(jnp.float32)
    return jnp.concatenate(parts, 0)


def sample_order():
    src, dst = iota((128, 128), 0), iota((128, 128), 1)
    hit = dst == (src % SAMPLES) * (128 // SAMPLES) + src // SAMPLES
    return jnp.where(hit, 1.0 / 8, 0.0).astype(jnp.bfloat16)


def table_of(tiles):
    lane, sub = iota((8, 128), 1), iota((8, 128), 0)
    tiles = list(tiles)
    for b in range(3):
        dist = 8 << b
        low = (lane & dist) == 0
        for j in range(8):
            if not j >> b & 1:
                one, two = tiles[j], tiles[j | 1 << b]
                tiles[j] = jnp.where(low, one, rolled(two, dist, 1))
                tiles[j | 1 << b] = jnp.where(low, rolled(one, -dist, 1), two)
    even, first = (sub & 1) == 0, lane < 64
    out = []
    for tile in tiles:
        far = rolled(tile, 64, 1)
        moved = jnp.where(even, rolled(far, -1, 0), rolled(far, 1, 0))
        out.append(jnp.where(even == first, tile, moved))
    return out


def box_of(own, before, after):
    lane = iota(own.shape, 1)
    first = lane < 64
    both = own + rolled(own, 64, 1)
    both = both + jnp.where(first, before + rolled(before, 64, 1), before)
    both = both + jnp.where(first, after, after + rolled(after, 64, 1))
    cell = lane & 63
    out = both
    for o in (-2, -1, 1, 2):
        valid = (cell + o >= 0) & (cell + o < 64)
        out = out + jnp.where(valid, rolled(both, -o, 1), 0.0)
    return out


def pick(places, values):
    return jnp.where(iota((192, 128), 0) & 63 == places, values, 0.0)


def picks(rank_a, rank_b, count):
    first = iota(rank_a.shape, 1) < 64
    low, high = jnp.minimum(rank_a, rank_b), jnp.maximum(rank_a, rank_b)
    couples = count * (count - 1) // 2
    place = ((low * (2 * count - 1 - low)) >> 1) + high - low - 1
    sign = jnp.where(first | (rank_a < rank_b), 1.0, -1.0)
    products = pick(place + jnp.where(first, 0, couples), sign)
    powers = pick(2 * couples + jnp.where(first, rank_a, rank_b), jnp.ones_like(sign))
    return products, powers


MESH = pl.DeviceIdType.MESH


def list_dates(pairs, dates, peers):
    length = pairs.shape[1]
    part = length // peers
    date = iota((dates, length), 0)
    named = (pairs[0:1] == date) | (pairs[1:2] == date)
    parts = iota((length, 128), 0) // part == iota((length, 128), 1)
    dims = (((1,), (0,)), ((), ()))
    one = jnp.bfloat16
    counts = lax.dot_general(
        named.astype(jnp.float32).astype(one),
        parts.astype(jnp.float32).astype(one),
        dims,
        preferred_element_type=jnp.float32,
    )
    needed = counts > 0.5
    before = iota((dates, dates), 1) < iota((dates, dates), 0)
    rank = lax.dot_general(
        before.astype(jnp.float32).astype(one),
        needed.astype(jnp.float32).astype(one),
        dims,
        preferred_element_type=jnp.float32,
    )
    rank = jnp.where(needed, rank, -1.0).astype(jnp.int32)
    date = iota(rank.shape, 0)
    rows = [jnp.sum(jnp.where(rank == k, date, 0), axis=0, keepdims=True) for k in range(peers)]
    return jnp.concatenate(rows, 0)


def stack_kernel(
    slc_ref,
    pairs_ref,
    table,
    boxed_ref,
    chosen,
    lines,
    sent,
    held,
    full,
    sums,
    tiles,
    halo,
    listed,
    ids,
    line_sem,
    send_a,
    recv_a,
    send_b,
    recv_b,
    send_h,
    recv_h,
    list_sem,
):
    peers, az_size = lax.axis_size("date"), lax.axis_size("az")
    me, az = lax.axis_index("date"), lax.axis_index("az")
    date_dev = slc_ref.shape[0]
    rounds = pairs_ref.shape[0]
    width = slc_ref.shape[3] // peers
    images_dev = 2 * date_dev
    sides = ((-1, az > 0), (1, az < az_size - 1))

    barrier = pltpu.get_barrier_semaphore()
    for o in range(1, peers):
        pl.semaphore_signal(
            barrier, inc=1, device_id={"date": lax.rem(me + o, peers)}, device_id_type=MESH
        )
    for step, there in sides:

        @pl.when(there)
        def _():
            pl.semaphore_signal(barrier, inc=1, device_id={"az": az + step}, device_id_type=MESH)

    def line(n):
        row = n % LINES * 2 + n // LINES
        return pltpu.make_async_copy(
            slc_ref.at[:, :, n, :], lines.at[:, :, row, :], line_sem.at[n]
        )

    for n in range(2 * LINES):
        line(n).start()
    for n in range(2 * LINES):
        line(n).wait()
    for j in range(peers):
        part = lines[:, :, :, j * width : (j + 1) * width]
        sent[j] = part.reshape(sent.shape[1:]).astype(jnp.bfloat16)
    greeted = peers - 1 + (az > 0).astype(jnp.int32) + (az < az_size - 1).astype(jnp.int32)
    pl.semaphore_wait(barrier, greeted)

    def images(o):
        peer = lax.rem(me + o, peers)
        return pltpu.make_async_remote_copy(
            src_ref=sent.at[peer],
            dst_ref=held.at[me],
            send_sem=send_a.at[o],
            recv_sem=recv_a.at[o],
            device_id={"date": peer},
            device_id_type=MESH,
        )

    for o in range(1, peers):
        images(o).start()
    for r in range(rounds):
        listed[r * peers : (r + 1) * peers, :] = list_dates(
            pairs_ref[r], date_dev * peers, peers
        )
    fetch = pltpu.make_async_copy(listed, ids, list_sem)
    fetch.start()
    order = sample_order()

    def take(owner, block):
        spread = jnp.dot(block, order, preferred_element_type=jnp.float32)
        at = pl.ds(owner * images_dev, images_dev)
        full[at] = spread.reshape((images_dev,) + full.shape[1:])

    take(me, sent[me])
    fetch.wait()
    lane = iota((1, 128), 1)
    for r in range(rounds):
        ranks = []
        for c in range(2):
            start = pl.multiple_of(me // 2 * 128, 128)
            near = pairs_ref[r, c : c + 1, pl.ds(start, 128)]
            own = jnp.where((lane < 64) == (lax.rem(me, 2) == 0), near, rolled(near, 64, 1))
            rank = jnp.zeros_like(own)
            for k in range(peers):
                rank = rank + (own > ids[r * peers + k, me]).astype(jnp.int32)
            ranks.append(rank)
        products, powers = picks(*ranks, peers)
        chosen[r, :128, :] = products.T.astype(jnp.bfloat16)
        chosen[r, 128:, :] = powers.T.astype(jnp.bfloat16)
    for o in range(1, peers):
        images(o).wait_recv()
        owner = lax.rem(me + peers - o, peers)
        take(owner, held[owner])

    def results(o, r):
        peer = lax.rem(me + o, peers)
        return pltpu.make_async_remote_copy(
            src_ref=sums.at[peer, r],
            dst_ref=tiles.at[me, r],
            send_sem=send_b.at[r, o],
            recv_sem=recv_b.at[r, o],
            device_id={"date": peer},
            device_id_type=MESH,
        )

    def serve(r, half, carry):
        for o in (2 * half + 1, 2 * half + 2):
            peer = lax.rem(me + o, peers)
            real, imag = [], []
            for k in range(peers):
                date = ids[r * peers + k, peer]
                real.append(full[2 * date])
                imag.append(full[2 * date + 1])
            sums[peer, r] = cell_sums(real, imag)

        results(2 * half + 1, r).start()

        @pl.when(half < peers // 2 - 1)
        def _():
            results(2 * half + 2, r).start()

        return carry

    for r in range(rounds):
        lax.fori_loop(0, peers // 2, functools.partial(serve, r), 0)
    tiles[me] = sums[me]

    def edge(n, step, r):
        return pltpu.make_async_remote_copy(
            src_ref=table.at[r],
            dst_ref=halo.at[n, r],
            send_sem=send_h.at[n, r],
            recv_sem=recv_h.at[n, r],
            device_id={"az": az + step},
            device_id_type=MESH,
        )

    for n, (step, there) in enumerate(sides):

        @pl.when(jnp.logical_not(there))
        def _():
            halo[1 - n] = jnp.zeros_like(halo[1 - n])

    for r in range(rounds):
        for o in range(1, peers):
            results(o, r).wait_recv()
        for k, tile in enumerate(table_of([tiles[j, r] for j in range(peers)])):
            table[r, 8 * k : 8 * k + 8, :] = tile
        for n, (step, there) in enumerate(sides):

            @pl.when(there)
            def _():
                edge(n, step, r).start()

    for r in range(rounds):
        for n, (step, there) in enumerate(sides):

            @pl.when(there)
            def _():
                edge(1 - n, step, r).wait_recv()

        boxed_ref[r] = box_of(table[r], halo[1, r], halo[0, r])

    for o in range(1, peers):
        images(o).wait_send()
        for r in range(rounds):
            results(o, r).wait_send()
    for n, (step, there) in enumerate(sides):

        @pl.when(there)
        def _():
            for r in range(rounds):
                edge(n, step, r).wait_send()


def pairs_kernel(table_ref, boxed_ref, chosen_ref, ifg_ref, coh_ref):
    for r in range(table_ref.shape[0]):
        means = jnp.dot(
            chosen_ref[r, :128, :], in_three(table_ref[r]), preferred_element_type=jnp.float32
        )
        for c in range(2):
            for row in range(2):
                part = means[64 * c : 64 * c + 64, 64 * row : 64 * row + 64]
                ifg_ref[pl.ds(256 * r + 2 * c + row, 64, stride=4), :] = part
        parts = jnp.dot(
            chosen_ref[r], in_three(boxed_ref[r]), preferred_element_type=jnp.float32
        )
        size = jnp.sqrt(parts[:64] * parts[:64] + parts[64:128] * parts[64:128])
        coherence = size / jnp.sqrt(parts[128:192] * parts[192:])
        for row in range(2):
            part = coherence[:, 64 * row : 64 * row + 64]
            coh_ref[pl.ds(128 * r + row, 64, stride=2), :] = part


def per_device_few(slc, pairs):
    peers = lax.axis_size("date")
    rounds = pairs.shape[0]
    pair_dev = pairs.shape[1] // peers
    date_dev, _, lines, columns = slc.shape
    width = columns // peers
    rows = date_dev * 2 * lines
    cells = columns // SAMPLES
    vmem = pl.BlockSpec(memory_space=pltpu.VMEM)
    dma = pltpu.SemaphoreType.DMA
    found = pl.pallas_call(
        stack_kernel,
        out_shape=(
            jax.ShapeDtypeStruct((rounds, 64, 128), jnp.float32),
            jax.ShapeDtypeStruct((rounds, 64, 128), jnp.float32),
            jax.ShapeDtypeStruct((rounds, 256, 192), jnp.bfloat16),
        ),
        in_specs=[pl.BlockSpec(memory_space=pl.ANY), vmem],
        out_specs=(vmem,) * 3,
        scratch_shapes=[
            pltpu.VMEM(slc.shape, jnp.float32),
            pltpu.VMEM((peers, rows, width), jnp.bfloat16),
            pltpu.VMEM((peers, rows, width), jnp.bfloat16),
            pltpu.VMEM((peers * date_dev * 2, lines, width), jnp.float32),
            pltpu.VMEM((peers, rounds, 8, 128), jnp.float32),
            pltpu.VMEM((peers, rounds, 8, 128), jnp.float32),
            pltpu.VMEM((2, rounds, 64, 128), jnp.float32),
            pltpu.VMEM((rounds * peers, 128), jnp.int32),
            pltpu.SMEM((rounds * peers, 128), jnp.int32),
            dma((lines,)),
            dma((peers,)),
            dma((peers,)),
            dma((rounds, peers)),
            dma((rounds, peers)),
            dma((2, rounds)),
            dma((2, rounds)),
            dma,
        ],
        compiler_params=pltpu.CompilerParams(collective_id=0, has_side_effects=True),
    )(slc, pairs.transpose(0, 2, 1))
    ifg, coh = pl.pallas_call(
        pairs_kernel,
        out_shape=(
            jax.ShapeDtypeStruct((rounds * pair_dev * 2 * lines // LINES, cells), jnp.float32),
            jax.ShapeDtypeStruct((rounds * pair_dev * lines // LINES, cells), jnp.float32),
        ),
        in_specs=[vmem] * 3,
        out_specs=(vmem, vmem),
    )(*found)
    return (
        ifg.reshape(rounds, pair_dev, 2, lines // LINES, cells),
        coh.reshape(rounds, pair_dev, lines // LINES, cells),
    )


def per_device(slc, pairs):
    peers = lax.axis_size("date")
    lines, columns = slc.shape[2:]
    pair_dev = pairs.shape[1] // peers
    few = (peers, pair_dev, lines, columns) == (8, 64, 2 * LINES, 64 * SAMPLES)
    return per_device_few(slc, pairs) if few else per_device_general(slc, pairs)


def solution(mesh):
    return jax.shard_map(
        per_device,
        mesh=mesh,
        in_specs=(P("date", None, "az", None), P()),
        out_specs=(P(None, "date", None, "az", None), P(None, "date", "az", None)),
        check_vma=False,
    )
```

```python
import jax
import jax.numpy as jnp
from jax import lax
from jax.experimental import pallas as pl
from jax.experimental.pallas import tpu as pltpu
from jax.sharding import PartitionSpec as P

CAP = 2


def with_halo(shard, sides, width):
    for axis, dim in sides:
        peers, length = (lax.axis_size(axis), shard.shape[dim])
        up = [(i, (i + 1) % peers) for i in range(peers - 1)]
        down = [(j, i) for i, j in up]
        last = lax.slice_in_dim(shard, length - width, length, axis=dim)
        first = lax.slice_in_dim(shard, 0, width, axis=dim)
        before = lax.ppermute(last, axis, up)
        after = lax.ppermute(first, axis, down)
        shard = jnp.concatenate([before, shard, after], axis=dim)
    return shard


def multilook(field):
    shape = field.shape
    blocks = field.reshape(shape[:-2] + (shape[-2] // 4, 4, shape[-1] // 16, 16))
    return blocks.mean(axis=(-3, -1))


def pair_looks(tiles):
    first = tiles[:, 0].astype(jnp.float32)
    second = tiles[:, 1].astype(jnp.float32)
    first_re, first_im = (first[:, 0], first[:, 1])
    second_re, second_im = (second[:, 0], second[:, 1])
    prod_re = first_re * second_re + first_im * second_im
    prod_im = first_im * second_re - first_re * second_im
    power_a = first_re * first_re + first_im * first_im
    power_b = second_re * second_re + second_im * second_im
    return jnp.stack(
        [multilook(prod_re), multilook(prod_im), multilook(power_a), multilook(power_b)], axis=1
    )


def coherence_from(padded):
    lines = padded.shape[-2] - 4
    columns = padded.shape[-1]
    az_sum = padded[..., 0:lines, :]
    for offset in range(1, 5):
        az_sum = az_sum + padded[..., offset : offset + lines, :]
    widths = [(0, 0)] * (az_sum.ndim - 1) + [(2, 2)]
    wide = jnp.pad(az_sum, widths)
    boxed = wide[..., 0:columns]
    for offset in range(1, 5):
        boxed = boxed + wide[..., offset : offset + columns]
    numer = jnp.sqrt(boxed[..., 0, :, :] ** 2 + boxed[..., 1, :, :] ** 2)
    return numer / jnp.sqrt(boxed[..., 2, :, :] * boxed[..., 3, :, :])


def per_device_general(slc, pairs):
    date_count = lax.axis_size("date")
    own_index = lax.axis_index("date")
    date_dev = slc.shape[0]
    pair_dev = pairs.shape[1] // date_count
    tile_shape = slc.shape[1:]
    quantized = lax.optimization_barrier(slc.astype(jnp.bfloat16))
    all_ids = jnp.arange(date_count * date_dev, dtype=jnp.int32)
    local_ids = own_index * date_dev + jnp.arange(date_dev, dtype=jnp.int32)
    local_pos = jnp.arange(date_dev, dtype=jnp.int32)
    slot_ids = jnp.arange(CAP, dtype=jnp.int32)
    looks_list = []
    for round_index in range(pairs.shape[0]):
        block = pairs[round_index]
        own_pairs = lax.dynamic_slice_in_dim(block, own_index * pair_dev, pair_dev, 0)
        entries = own_pairs.reshape(-1)
        wanted = block.reshape(date_count, 2 * pair_dev)
        needed = jnp.any(wanted[:, :, None] == local_ids[None, None, :], axis=1).astype(jnp.int32)
        ranks = jnp.cumsum(needed, axis=1) - needed
        picked = needed[:, None, :] * (ranks[:, None, :] == slot_ids[None, :, None]).astype(
            jnp.int32
        )
        source_local = jnp.sum(picked * local_pos[None, None, :], axis=2)
        present = jnp.sum(picked, axis=2) > 0
        outgoing = jnp.take(quantized, source_local.reshape(-1), axis=0).reshape(
            (date_count, CAP) + tile_shape
        )
        outgoing = jnp.where(present[:, :, None, None, None], outgoing, jnp.zeros((), jnp.bfloat16))
        incoming = lax.all_to_all(outgoing, "date", split_axis=0, concat_axis=0, tiled=True)
        matches = entries[:, None] == all_ids[None, :]
        my_need = jnp.any(matches, axis=0).astype(jnp.int32).reshape(date_count, date_dev)
        my_rank = (jnp.cumsum(my_need, axis=1) - my_need).reshape(-1)
        entry_slot = jnp.sum(jnp.where(matches, my_rank[None, :], 0), axis=1)
        position = entries // date_dev * CAP + entry_slot
        fetched = jnp.take(incoming.reshape((date_count * CAP,) + tile_shape), position, axis=0)
        looks = pair_looks(fetched.reshape((pair_dev, 2) + tile_shape))
        looks_list.append(looks)
    stacked = jnp.stack(looks_list, axis=0)
    padded = with_halo(stacked, (("az", 3),), 2)
    coherence = coherence_from(padded)
    interferogram = stacked[:, :, 0:2]
    return (interferogram, coherence)


LINES, SAMPLES = 4, 16
STEPS = ((0, 2, 2), (0, 2, 1), (1, 8, 8), (1, 8, 4), (1, 8, 2), (1, 8, 1))


def iota(shape, dim):
    return lax.broadcasted_iota(jnp.int32, shape, dim)


def place_of(leaf):
    bit = [(leaf >> n) & 1 for n in range(6)]
    return 32 * bit[3] + 16 * bit[4] + 8 * bit[5] + 4 * bit[0] + 2 * bit[1] + bit[2]


def rolled(x, shift, dim):
    return pltpu.roll(x, shift % x.shape[dim], dim)


def join(one, two, dim, unit, dist, phase):
    low = ((iota(one.shape, dim) - unit * phase) & (unit * dist)) == 0
    kept = jnp.where(low, one, two)
    other = jnp.where(low, two, one)
    return kept + rolled(other, -unit * dist, dim)


def cell_sums(real, imag):
    count = len(real)
    couples = [(i, j) for i in range(count) for j in range(i + 1, count)]

    def quantity(place):
        if place < len(couples):
            i, j = couples[place]
            return real[i] * real[j] + imag[i] * imag[j]
        place -= len(couples)
        if place < len(couples):
            i, j = couples[place]
            return imag[i] * real[j] - real[i] * imag[j]
        i = place - len(couples)
        return real[i] * real[i] + imag[i] * imag[i]

    def build(level, base, phases):
        if level == 0:
            return quantity(place_of(base))
        dim, unit, dist = STEPS[level - 1]
        moved = tuple(p + dist if d == dim else p for d, p in enumerate(phases))
        one = build(level - 1, base, phases)
        two = build(level - 1, base + (1 << (level - 1)), moved)
        return join(one, two, dim, unit, dist, phases[dim])

    return build(len(STEPS), 0, (0, 0))


def in_three(x):
    parts = []
    for _ in range(3):
        part = x.astype(jnp.bfloat16)
        parts.append(part)
        x = x - part.astype(jnp.float32)
    return jnp.concatenate(parts, 0)


def sample_order():
    src, dst = iota((128, 128), 0), iota((128, 128), 1)
    hit = dst == (src % SAMPLES) * (128 // SAMPLES) + src // SAMPLES
    return jnp.where(hit, 1.0 / 8, 0.0).astype(jnp.bfloat16)


def table_of(tiles):
    lane, sub = iota((8, 128), 1), iota((8, 128), 0)
    tiles = list(tiles)
    for b in range(3):
        dist = 8 << b
        low = (lane & dist) == 0
        for j in range(8):
            if not j >> b & 1:
                one, two = tiles[j], tiles[j | 1 << b]
                tiles[j] = jnp.where(low, one, rolled(two, dist, 1))
                tiles[j | 1 << b] = jnp.where(low, rolled(one, -dist, 1), two)
    even, first = (sub & 1) == 0, lane < 64
    out = []
    for tile in tiles:
        far = rolled(tile, 64, 1)
        moved = jnp.where(even, rolled(far, -1, 0), rolled(far, 1, 0))
        out.append(jnp.where(even == first, tile, moved))
    return out


def box_of(own, before, after):
    lane = iota(own.shape, 1)
    first = lane < 64
    both = own + rolled(own, 64, 1)
    both = both + jnp.where(first, before + rolled(before, 64, 1), before)
    both = both + jnp.where(first, after, after + rolled(after, 64, 1))
    cell = lane & 63
    out = both
    for o in (-2, -1, 1, 2):
        valid = (cell + o >= 0) & (cell + o < 64)
        out = out + jnp.where(valid, rolled(both, -o, 1), 0.0)
    return out


def pick(places, values):
    return jnp.where(iota((192, 128), 0) & 63 == places, values, 0.0)


def picks(rank_a, rank_b, count):
    first = iota(rank_a.shape, 1) < 64
    low, high = jnp.minimum(rank_a, rank_b), jnp.maximum(rank_a, rank_b)
    couples = count * (count - 1) // 2
    place = ((low * (2 * count - 1 - low)) >> 1) + high - low - 1
    sign = jnp.where(first | (rank_a < rank_b), 1.0, -1.0)
    products = pick(place + jnp.where(first, 0, couples), sign)
    powers = pick(2 * couples + jnp.where(first, rank_a, rank_b), jnp.ones_like(sign))
    return products, powers


MESH = pl.DeviceIdType.MESH


def list_dates(pairs, dates, peers):
    length = pairs.shape[1]
    part = length // peers
    date = iota((dates, length), 0)
    named = (pairs[0:1] == date) | (pairs[1:2] == date)
    parts = iota((length, 128), 0) // part == iota((length, 128), 1)
    dims = (((1,), (0,)), ((), ()))
    one = jnp.bfloat16
    counts = lax.dot_general(
        named.astype(jnp.float32).astype(one),
        parts.astype(jnp.float32).astype(one),
        dims,
        preferred_element_type=jnp.float32,
    )
    needed = counts > 0.5
    before = iota((dates, dates), 1) < iota((dates, dates), 0)
    rank = lax.dot_general(
        before.astype(jnp.float32).astype(one),
        needed.astype(jnp.float32).astype(one),
        dims,
        preferred_element_type=jnp.float32,
    )
    rank = jnp.where(needed, rank, -1.0).astype(jnp.int32)
    date = iota(rank.shape, 0)
    rows = [jnp.sum(jnp.where(rank == k, date, 0), axis=0, keepdims=True) for k in range(peers)]
    return jnp.concatenate(rows, 0)


def stack_kernel(
    slc_ref,
    pairs_ref,
    table,
    boxed_ref,
    chosen,
    lines,
    sent,
    held,
    full,
    sums,
    tiles,
    halo,
    listed,
    ids,
    line_sem,
    send_a,
    recv_a,
    send_b,
    recv_b,
    send_h,
    recv_h,
    list_sem,
):
    peers, az_size = lax.axis_size("date"), lax.axis_size("az")
    me, az = lax.axis_index("date"), lax.axis_index("az")
    date_dev = slc_ref.shape[0]
    rounds = pairs_ref.shape[0]
    width = slc_ref.shape[3] // peers
    images_dev = 2 * date_dev
    sides = ((-1, az > 0), (1, az < az_size - 1))

    barrier = pltpu.get_barrier_semaphore()
    for o in range(1, peers):
        pl.semaphore_signal(
            barrier, inc=1, device_id={"date": lax.rem(me + o, peers)}, device_id_type=MESH
        )
    for step, there in sides:

        @pl.when(there)
        def _():
            pl.semaphore_signal(barrier, inc=1, device_id={"az": az + step}, device_id_type=MESH)

    def line(n):
        return pltpu.make_async_copy(slc_ref.at[n], lines.at[n], line_sem.at[n])

    for n in range(date_dev):
        line(n).start()
    rows_date = sent.shape[1] // date_dev
    for n in range(date_dev):
        line(n).wait()
        for j in range(peers):
            part = lines[n, :, :, j * width : (j + 1) * width]
            at = slice(n * rows_date, (n + 1) * rows_date)
            sent[j, at] = part.reshape(rows_date, width).astype(jnp.bfloat16)
    greeted = peers - 1 + (az > 0).astype(jnp.int32) + (az < az_size - 1).astype(jnp.int32)
    pl.semaphore_wait(barrier, greeted)

    def images(o):
        peer = lax.rem(me + o, peers)
        return pltpu.make_async_remote_copy(
            src_ref=sent.at[peer],
            dst_ref=held.at[me],
            send_sem=send_a.at[o],
            recv_sem=recv_a.at[o],
            device_id={"date": peer},
            device_id_type=MESH,
        )

    for o in range(1, peers):
        images(o).start()
    for r in range(rounds):
        listed[r * peers : (r + 1) * peers, :] = list_dates(
            pairs_ref[r], date_dev * peers, peers
        )
    fetch = pltpu.make_async_copy(listed, ids, list_sem)
    fetch.start()
    order = sample_order()

    def take(owner, block):
        spread = jnp.dot(block, order, preferred_element_type=jnp.float32)
        for image in range(images_dev):
            for group in range(2):
                row = image * 8 + group * LINES
                at = (owner * images_dev + image, pl.ds(group, LINES, stride=2))
                full[at] = spread[row : row + LINES]

    take(me, sent[me])
    fetch.wait()
    lane = iota((1, 128), 1)
    for r in range(rounds):
        ranks = []
        for c in range(2):
            start = pl.multiple_of(me // 2 * 128, 128)
            near = pairs_ref[r, c : c + 1, pl.ds(start, 128)]
            own = jnp.where((lane < 64) == (lax.rem(me, 2) == 0), near, rolled(near, 64, 1))
            rank = jnp.zeros_like(own)
            for k in range(peers):
                rank = rank + (own > ids[r * peers + k, me]).astype(jnp.int32)
            ranks.append(rank)
        products, powers = picks(*ranks, peers)
        chosen[r, :128, :] = products.T.astype(jnp.bfloat16)
        chosen[r, 128:, :] = powers.T.astype(jnp.bfloat16)
    for o in range(1, peers):
        images(o).wait_recv()
        owner = lax.rem(me + peers - o, peers)
        take(owner, held[owner])

    def results(o):
        peer = lax.rem(me + o, peers)
        return pltpu.make_async_remote_copy(
            src_ref=sums.at[peer],
            dst_ref=tiles.at[me],
            send_sem=send_b.at[o],
            recv_sem=recv_b.at[o],
            device_id={"date": peer},
            device_id_type=MESH,
        )

    def serve(o, carry):
        peer = lax.rem(me + o, peers)
        for r in range(rounds):
            real, imag = [], []
            for k in range(peers):
                date = ids[r * peers + k, peer]
                real.append(full[2 * date])
                imag.append(full[2 * date + 1])
            sums[peer, r] = cell_sums(real, imag)

        @pl.when(o < peers)
        def _():
            results(o).start()

        return carry

    lax.fori_loop(1, peers + 1, serve, 0)
    tiles[me] = sums[me]
    for o in range(1, peers):
        results(o).wait_recv()
    for r in range(rounds):
        for k, tile in enumerate(table_of([tiles[j, r] for j in range(peers)])):
            table[r, 8 * k : 8 * k + 8, :] = tile

    def edge(n, step):
        return pltpu.make_async_remote_copy(
            src_ref=table,
            dst_ref=halo.at[n],
            send_sem=send_h.at[n],
            recv_sem=recv_h.at[n],
            device_id={"az": az + step},
            device_id_type=MESH,
        )

    for n, (step, there) in enumerate(sides):

        @pl.when(there)
        def _():
            edge(n, step).start()

        @pl.when(jnp.logical_not(there))
        def _():
            halo[1 - n] = jnp.zeros_like(halo[1 - n])

    for n, (step, there) in enumerate(sides):

        @pl.when(there)
        def _():
            edge(1 - n, step).wait_recv()

    for r in range(rounds):
        boxed_ref[r] = box_of(table[r], halo[1, r], halo[0, r])

    for o in range(1, peers):
        images(o).wait_send()
        results(o).wait_send()
    for n, (step, there) in enumerate(sides):

        @pl.when(there)
        def _():
            edge(n, step).wait_send()


def pairs_kernel(table_ref, boxed_ref, chosen_ref, ifg_ref, coh_ref):
    for r in range(table_ref.shape[0]):
        means = jnp.dot(
            chosen_ref[r, :128, :], in_three(table_ref[r]), preferred_element_type=jnp.float32
        )
        for c in range(2):
            for row in range(2):
                part = means[64 * c : 64 * c + 64, 64 * row : 64 * row + 64]
                ifg_ref[pl.ds(256 * r + 2 * c + row, 64, stride=4), :] = part
        parts = jnp.dot(
            chosen_ref[r], in_three(boxed_ref[r]), preferred_element_type=jnp.float32
        )
        size = jnp.sqrt(parts[:64] * parts[:64] + parts[64:128] * parts[64:128])
        coherence = size / jnp.sqrt(parts[128:192] * parts[192:])
        for row in range(2):
            part = coherence[:, 64 * row : 64 * row + 64]
            coh_ref[pl.ds(128 * r + row, 64, stride=2), :] = part


def per_device_few(slc, pairs):
    peers = lax.axis_size("date")
    rounds = pairs.shape[0]
    pair_dev = pairs.shape[1] // peers
    date_dev, _, lines, columns = slc.shape
    width = columns // peers
    rows = date_dev * 2 * lines
    cells = columns // SAMPLES
    vmem = pl.BlockSpec(memory_space=pltpu.VMEM)
    dma = pltpu.SemaphoreType.DMA
    found = pl.pallas_call(
        stack_kernel,
        out_shape=(
            jax.ShapeDtypeStruct((rounds, 64, 128), jnp.float32),
            jax.ShapeDtypeStruct((rounds, 64, 128), jnp.float32),
            jax.ShapeDtypeStruct((rounds, 256, 192), jnp.bfloat16),
        ),
        in_specs=[pl.BlockSpec(memory_space=pl.ANY), vmem],
        out_specs=(vmem,) * 3,
        scratch_shapes=[
            pltpu.VMEM(slc.shape, jnp.float32),
            pltpu.VMEM((peers, rows, width), jnp.bfloat16),
            pltpu.VMEM((peers, rows, width), jnp.bfloat16),
            pltpu.VMEM((peers * date_dev * 2, lines, width), jnp.float32),
            pltpu.VMEM((peers, rounds, 8, 128), jnp.float32),
            pltpu.VMEM((peers, rounds, 8, 128), jnp.float32),
            pltpu.VMEM((2, rounds, 64, 128), jnp.float32),
            pltpu.VMEM((rounds * peers, 128), jnp.int32),
            pltpu.SMEM((rounds * peers, 128), jnp.int32),
            dma((date_dev,)),
            dma((peers,)),
            dma((peers,)),
            dma((peers,)),
            dma((peers,)),
            dma((2,)),
            dma((2,)),
            dma,
        ],
        compiler_params=pltpu.CompilerParams(collective_id=0, has_side_effects=True),
    )(slc, pairs.transpose(0, 2, 1))
    ifg, coh = pl.pallas_call(
        pairs_kernel,
        out_shape=(
            jax.ShapeDtypeStruct((rounds * pair_dev * 2 * lines // LINES, cells), jnp.float32),
            jax.ShapeDtypeStruct((rounds * pair_dev * lines // LINES, cells), jnp.float32),
        ),
        in_specs=[vmem] * 3,
        out_specs=(vmem, vmem),
    )(*found)
    return (
        ifg.reshape(rounds, pair_dev, 2, lines // LINES, cells),
        coh.reshape(rounds, pair_dev, lines // LINES, cells),
    )


def per_device(slc, pairs):
    peers = lax.axis_size("date")
    lines, columns = slc.shape[2:]
    pair_dev = pairs.shape[1] // peers
    few = (peers, pair_dev, lines, columns) == (8, 64, 2 * LINES, 64 * SAMPLES)
    return per_device_few(slc, pairs) if few else per_device_general(slc, pairs)


def solution(mesh):
    return jax.shard_map(
        per_device,
        mesh=mesh,
        in_specs=(P("date", None, "az", None), P()),
        out_specs=(P(None, "date", None, "az", None), P(None, "date", "az", None)),
        check_vma=False,
    )
```
